32 devices in a mesh: groups: 2 (over x), tm: 8 (over z, y), space: 2 (over core).
Axes of the slice: x: 2, y: 2, z: 4, core: 2. Of those that a mesh axis runs over, the one named last changes fastest.
Arguments:
- frames_in: bfloat16 [16, 32, 80, 2240], P(('groups', 'tm'), 'space'), parts along dimension 0, may hold values from -6 to 6
- queries: bfloat16 [16, 32, 80, 1120], P(('groups', 'tm'), 'space'), parts along dimension 0, may hold values from -6 to 6
- key_weight: bfloat16 [2240, 1120], replicated, may hold values from -0.125 to 0.125
- value_weight: bfloat16 [2240, 1120], replicated, may hold values from -0.125 to 0.125
- conv_weight: float32 [9, 1120], replicated, may hold values from -2 to 2
- norm_gain: float32 [1120], replicated, may hold values from 0.1 to 1.9
Outputs:
- mixed: bfloat16 [16, 32, 80, 1120], P(('groups', 'tm'), 'space'), parts along dimension 0
The draws below stay inside these ranges and needn't reach their ends.
There are 2 independent parts, one for each index of `groups`. The reference program is written for one: setup_inputs(seed, part) draws one part's arguments, and reference() takes and returns one part's arrays. A program takes and returns all parts, laid end to end along the dimension named above; an argument that names none is the same for every part. Nothing has to cross between parts.
All inputs are finite; a program needn't handle non-finite values.
Results may differ from the reference program's by a relative error of at most 0.005.
Values may be sent and summed in bfloat16 or wider, within the bound.
No kernel may reach another device: no remote copies, remote signals or barrier semaphores. Data moves between devices by JAX's collectives and lax.ppermute only.
A program may use at most 192 MiB of HBM per device.

```python
import jax
import jax.numpy as jnp
from jax import lax

D = 2240
HEADS = 10
HEAD = 112
FW = 80
HD = 1120
FH = 32
FRAMES = 8


def levels(own_key, shape, split, low, largest):
    gain, own = 1.0, jax.random.fold_in(own_key, 6)
    for position, blocks in split:
        heights = jnp.exp(jax.random.uniform(jax.random.fold_in(own, position), (blocks,), jnp.float32, low / len(split), largest / len(split)))
        gain = gain * jnp.repeat(heights, shape[position] // blocks).reshape([-1 if axis == position else 1 for axis in range(len(shape))])
    return gain


def gaussian(key, shape, scale, most, split=(), kind=jnp.bfloat16):
    array = scale * jax.random.normal(key, shape, jnp.float32)
    if split:
        array = array * levels(key, shape, split, -0.22, 0.18)
    return jnp.clip(array, -most, most).astype(kind)


def setup_inputs(seed: int = 0, part: int = 0) -> dict:
    streams_of = jax.random.split(jax.random.key(seed), 7)
    part_splits = jax.random.split(jax.random.fold_in(streams_of[6], part), 7)
    return {
        "frames_in": gaussian(part_splits[0], (FRAMES, FH, FW, D), 1.0, 6.0, ((0, 8), (1, 2))),
        "queries": gaussian(part_splits[1], (FRAMES, FH, FW, HD), 1.0, 6.0, ((0, 8), (1, 2))),
        "key_weight": gaussian(streams_of[2], (D, HD), D ** -0.5, 0.125),
        "value_weight": gaussian(streams_of[3], (D, HD), D ** -0.5, 0.125),
        "conv_weight": gaussian(streams_of[4], (9, HD), 9 ** -0.5, 2.0, (), jnp.float32),
        "norm_gain": jnp.clip(1.0 + 0.18 * jax.random.normal(streams_of[5], (HD,), jnp.float32), 0.1, 1.9),
    }


def feature_map(a):
    return jnp.where(a > 0, a + 1.0, jnp.exp(jnp.minimum(a, 0.0)))

def reference(frames_in, queries, key_weight, value_weight, conv_weight, norm_gain):
    frames, height, width, model = frames_in.shape
    inner = key_weight.shape[1]
    flat = frames_in.reshape(-1, model)
    keys = feature_map(jnp.dot(flat, key_weight, preferred_element_type=jnp.float32)).astype(jnp.bfloat16)
    values = jnp.dot(flat, value_weight, preferred_element_type=jnp.float32).astype(jnp.bfloat16)
    key_heads = keys.reshape(frames, height * width, HEADS, HEAD).astype(jnp.float32)
    value_heads = values.reshape(frames, height * width, HEADS, HEAD).astype(jnp.float32)
    frame_state = jnp.einsum('ftha,fthb->fhab', key_heads, value_heads, precision=lax.Precision.HIGHEST)
    prefix = jnp.cumsum(frame_state, axis=0)
    qfeat = feature_map(queries.astype(jnp.float32)).reshape(frames, height * width, HEADS, HEAD)
    attn = jnp.einsum('ftha,fhab->fthb', qfeat, prefix, precision=lax.Precision.HIGHEST)
    scale = lax.rsqrt(lax.optimization_barrier(jnp.mean(attn * attn, axis=-1, keepdims=True)) + 1e-06)
    normed = (attn * scale).reshape(frames, height, width, inner) * norm_gain
    image = values.reshape(frames, height, width, inner).astype(jnp.float32)
    padded = jnp.pad(image, ((0, 0), (1, 1), (1, 1), (0, 0)))
    local = jnp.zeros_like(image)
    for row_off in range(3):
        for col_off in range(3):
            local = local + conv_weight[row_off * 3 + col_off] * padded[:, row_off:row_off + height, col_off:col_off + width, :]
    return (normed + local).astype(jnp.bfloat16)
```

```python
import functools

import jax
import jax.numpy as jnp
from jax import lax
from jax.experimental import pallas as pl
from jax.experimental.pallas import tpu as pltpu
from jax.sharding import PartitionSpec as P

HEADS = 10
HEAD = 112
TILE = 256
F32 = jnp.float32
BF16 = jnp.bfloat16
MIB = 1 << 20


def feature_map(a):
    return jnp.where(a > 0, a + 1.0, jnp.exp(jnp.minimum(a, 0.0)))


def first_head(tile, inner):
    return min(tile * TILE // HEAD, inner // HEAD - 4)


def project_kernel(
    core_ref, x_ref, wk_ref, wv_ref, v_ref, mine_ref, send_ref, edge_ref, kt, vs, state, *, chunk, width
):
    j = pl.program_id(0)
    steps = pl.num_programs(0)
    count = x_ref.shape[0]
    inner = state.shape[1]
    last_head = inner // HEAD - 4

    def one(m, carry):
        at = pl.multiple_of(m * chunk, chunk)
        rows = pl.ds(at, chunk)
        x = x_ref[rows, :]
        k = feature_map(jnp.dot(x, wk_ref[...], preferred_element_type=F32)).astype(BF16)
        kt[pl.ds(pl.multiple_of(j * TILE, TILE), TILE), rows] = k.T
        v = jnp.dot(x, wv_ref[...], preferred_element_type=F32).astype(BF16)
        v_ref[rows, :] = v
        vs[j, rows, :] = v
        return carry

    lax.fori_loop(0, count // chunk, one, 0)

    def state_tile(i):
        head = jnp.minimum(2 * i, last_head)
        keys = kt[pl.ds(pl.multiple_of(head * HEAD, 16), 4 * HEAD), :]
        full = jnp.dot(keys, vs[i], preferred_element_type=F32)
        column = lax.broadcasted_iota(jnp.int32, (HEAD, TILE), 1) + i * TILE
        total = jnp.zeros((HEAD, TILE), F32)
        for m in range(4):
            low = (head + m) * HEAD
            inside = (column >= low) & (column < low + HEAD)
            total = total + jnp.where(inside, full[m * HEAD : (m + 1) * HEAD, :], 0.0)
        return total

    def keep(i, total):
        for t in range(inner // TILE):

            @pl.when(i == t)
            def _():
                state[:, t * TILE : (t + 1) * TILE] = total

    @pl.when(j > 0)
    def _():
        keep(j - 1, state_tile(j - 1))

    @pl.when(j == steps - 1)
    def _():
        rest = inner - inner // TILE * TILE
        state[:, inner - rest :] = state_tile(j)[:, :rest]
        core = core_ref[0]
        half = HEAD // 2
        mine_ref[...] = state[pl.ds(pl.multiple_of(core * half, 8), half), :]
        send_ref[...] = state[pl.ds(pl.multiple_of((1 - core) * half, 8), half), :].astype(BF16)
        start = pl.multiple_of((1 - core) * (count - width), 16)
        for t in range(inner // TILE):
            edge_ref[:, t * TILE : (t + 1) * TILE] = vs[t, pl.ds(start, width), :]
        edge_ref[:, inner - rest :] = vs[inner // TILE, pl.ds(start, width), :rest]


def project(core, flat, key_weight, value_weight, width):
    count, model = flat.shape
    inner = key_weight.shape[1]
    steps = pl.cdiv(inner, TILE)
    half = HEAD // 2
    return pl.pallas_call(
        functools.partial(project_kernel, chunk=256, width=width),
        grid_spec=pltpu.PrefetchScalarGridSpec(
            num_scalar_prefetch=1,
            grid=(steps,),
            in_specs=[
                pl.BlockSpec((count, model), lambda j, c: (0, 0)),
                pl.BlockSpec((model, TILE), lambda j, c: (0, j)),
                pl.BlockSpec((model, TILE), lambda j, c: (0, j)),
            ],
            out_specs=[
                pl.BlockSpec((count, TILE), lambda j, c: (0, j)),
                pl.BlockSpec((half, inner), lambda j, c: (0, 0)),
                pl.BlockSpec((half, inner), lambda j, c: (0, 0)),
                pl.BlockSpec((width, inner), lambda j, c: (0, 0)),
            ],
            scratch_shapes=[
                pltpu.VMEM((steps * TILE, count), BF16),
                pltpu.VMEM((steps, count, TILE), BF16),
                pltpu.VMEM((HEAD, inner), F32),
            ],
        ),
        out_shape=[
            jax.ShapeDtypeStruct((count, inner), BF16),
            jax.ShapeDtypeStruct((half, inner), F32),
            jax.ShapeDtypeStruct((half, inner), BF16),
            jax.ShapeDtypeStruct((width, inner), BF16),
        ],
        compiler_params=pltpu.CompilerParams(vmem_limit_bytes=50 * MIB),
        cost_estimate=pl.CostEstimate(
            flops=4 * count * model * inner, bytes_accessed=2 * (count * model + 2 * model * inner), transcendentals=0
        ),
        name="project",
    )(core, flat, key_weight, value_weight)


def local_kernel(core_ref, v_ref, halo_ref, q_ref, w_ref, local_ref, qf_ref, ext, *, width, rows):
    i = pl.program_id(0)
    count, inner = v_ref.shape

    @pl.when(i == 0)
    def _():
        core = core_ref[0]
        halo = halo_ref[...]
        nothing = jnp.zeros_like(halo)
        ext[0:width, :] = jnp.where(core == 1, halo, nothing)
        ext[width : width + count, :] = v_ref[...]
        ext[width + count :, :] = jnp.where(core == 0, halo, nothing)

    lanes = [(a, min(a + 128, inner)) for a in range(0, inner, 128)]

    def row(r, carry):
        at = pl.multiple_of((i * rows + r) * width, 16)
        here = pl.ds(pl.multiple_of(r * width, 16), width)
        for low, high in lanes:
            taps = [ext[pl.ds(at + d * width, width), low:high].astype(F32) for d in range(3)]
            side = []
            for c in range(3):
                acc = taps[0] * w_ref[c : c + 1, low:high]
                acc = acc + taps[1] * w_ref[3 + c : 4 + c, low:high]
                side.append(acc + taps[2] * w_ref[6 + c : 7 + c, low:high])
            place = lax.broadcasted_iota(jnp.int32, side[0].shape, 0)
            left = jnp.where(place > 0, pltpu.roll(side[0], 1, 0), 0.0)
            right = jnp.where(place < width - 1, pltpu.roll(side[2], width - 1, 0), 0.0)
            local_ref[here, low:high] = side[1] + left + right
            qf_ref[here, low:high] = feature_map(q_ref[here, low:high].astype(F32)).astype(BF16)
        return carry

    lax.fori_loop(0, rows, row, 0)


def local_branch(core, values, halo, queries, conv_weight, width):
    count, inner = values.shape
    rows = 4
    block = rows * width
    return pl.pallas_call(
        functools.partial(local_kernel, width=width, rows=rows),
        grid_spec=pltpu.PrefetchScalarGridSpec(
            num_scalar_prefetch=1,
            grid=(count // block,),
            in_specs=[
                pl.BlockSpec((count, inner), lambda i, c: (0, 0)),
                pl.BlockSpec((width, inner), lambda i, c: (0, 0)),
                pl.BlockSpec((block, inner), lambda i, c: (i, 0)),
                pl.BlockSpec(conv_weight.shape, lambda i, c: (0, 0)),
            ],
            out_specs=[
                pl.BlockSpec((block, inner), lambda i, c: (i, 0)),
                pl.BlockSpec((block, inner), lambda i, c: (i, 0)),
            ],
            scratch_shapes=[pltpu.VMEM((count + 2 * width, inner), BF16)],
        ),
        out_shape=[
            jax.ShapeDtypeStruct((count, inner), F32),
            jax.ShapeDtypeStruct((count, inner), BF16),
        ],
        compiler_params=pltpu.CompilerParams(vmem_limit_bytes=32 * MIB),
        cost_estimate=pl.CostEstimate(
            flops=20 * count * inner, bytes_accessed=12 * count * inner, transcendentals=count * inner
        ),
        name="local_branch",
    )(core, values, halo, queries, conv_weight)


def attend_kernel(p_ref, qf_ref, local_ref, gain_ref, out_ref, band, ones):
    inner = p_ref.shape[1]
    heads = inner // HEAD

    @pl.when(pl.program_id(0) == 0)
    def _():
        p = p_ref[...]
        column = lax.broadcasted_iota(jnp.int32, p.shape, 1)
        for h in range(heads):
            inside = (column >= h * HEAD) & (column < (h + 1) * HEAD)
            band[h * HEAD : (h + 1) * HEAD, :] = jnp.where(inside, p, jnp.zeros_like(p))
            ones[h * HEAD : (h + 1) * HEAD, :] = inside.astype(F32).astype(BF16)

    tiles = [(a, min(a + TILE, inner)) for a in range(0, inner, TILE)]
    spans = []
    for low, high in tiles:
        start = low // HEAD * HEAD // 128 * 128
        stop = min(-(-(-(-high // HEAD) * HEAD) // 128) * 128, inner)
        spans.append((start, stop))
    attn = []
    for (low, high), (start, stop) in zip(tiles, spans):
        attn.append(jnp.dot(qf_ref[:, start:stop], band[start:stop, low:high], preferred_element_type=F32))
    attn = jnp.concatenate(attn, axis=1)
    square = (attn * attn).astype(BF16)
    for (low, high), (start, stop) in zip(tiles, spans):
        total = jnp.dot(square[:, start:stop], ones[start:stop, low:high], preferred_element_type=F32)
        scale = lax.rsqrt(total * (1.0 / HEAD) + 1e-06)
        normed = attn[:, low:high] * scale * gain_ref[:, low:high]
        out_ref[:, low:high] = (normed + local_ref[:, low:high]).astype(BF16)


def attend(prefix, qfeat, local, gain):
    count, inner = qfeat.shape
    block = 256
    return pl.pallas_call(
        attend_kernel,
        grid=(count // block,),
        in_specs=[
            pl.BlockSpec((HEAD, inner), lambda i: (0, 0)),
            pl.BlockSpec((block, inner), lambda i: (i, 0)),
            pl.BlockSpec((block, inner), lambda i: (i, 0)),
            pl.BlockSpec((1, inner), lambda i: (0, 0)),
        ],
        out_specs=pl.BlockSpec((block, inner), lambda i: (i, 0)),
        scratch_shapes=[pltpu.VMEM((inner, inner), BF16), pltpu.VMEM((inner, inner), BF16)],
        out_shape=jax.ShapeDtypeStruct((count, inner), BF16),
        compiler_params=pltpu.CompilerParams(vmem_limit_bytes=32 * MIB),
        cost_estimate=pl.CostEstimate(
            flops=4 * count * inner * 512, bytes_accessed=8 * count * inner, transcendentals=count * inner
        ),
        name="attend",
    )(prefix, qfeat, local, gain)


def swapped(block, axis, bit):
    return lax.ppermute(block, axis, [(i, i ^ bit) for i in range(lax.axis_size(axis))])


def shards(frames_in, queries, key_weight, value_weight, conv_weight, norm_gain):
    _, rows, width, model = frames_in.shape
    inner = key_weight.shape[1]
    count = rows * width
    core_index = lax.axis_index("space")
    frame = lax.axis_index("tm")
    core = core_index.astype(jnp.int32).reshape(1)
    values, mine, send, edge = project(core, frames_in.reshape(count, model), key_weight, value_weight, width)
    total = mine + swapped(send, "space", 1).astype(F32)
    halo = swapped(edge, "space", 1)
    local, qfeat = local_branch(core, values, halo, queries.reshape(count, inner), conv_weight, width)
    prefix = total
    bit = 1
    while bit < lax.axis_size("tm"):
        other = swapped(total.astype(BF16), "tm", bit).astype(F32)
        prefix = prefix + jnp.where(frame & bit != 0, other, 0.0)
        total = total + other
        bit *= 2
    prefix = prefix.astype(BF16)
    pair = swapped(prefix, "space", 1)
    low = jnp.where(core_index == 0, prefix, pair)
    high = jnp.where(core_index == 0, pair, prefix)
    whole = jnp.concatenate([low, high], axis=0)
    mixed = attend(whole, qfeat, local, norm_gain.reshape(1, inner))
    return mixed.reshape(1, rows, width, inner)


def solution(mesh):
    in_specs = (
        P(("groups", "tm"), "space", None, None),
        P(("groups", "tm"), "space", None, None),
        P(),
        P(),
        P(),
        P(),
    )
    out_specs = P(("groups", "tm"), "space", None, None)
    return jax.shard_map(shards, mesh=mesh, in_specs=in_specs, out_specs=out_specs, check_vma=False)
```

```python
import functools

import jax
import jax.numpy as jnp
from jax import lax
from jax.experimental import pallas as pl
from jax.experimental.pallas import tpu as pltpu
from jax.sharding import PartitionSpec as P

HEAD = 112
TILE = 256
FIRST = 2 * TILE
F32 = jnp.float32
BF16 = jnp.bfloat16
MIB = 1 << 20
VMEM = pl.BlockSpec(memory_space=pltpu.VMEM)
SMEM = pl.BlockSpec(memory_space=pltpu.SMEM)


def feature_map(a):
    return jnp.where(a > 0, a + 1.0, jnp.exp(jnp.minimum(a, 0.0)))


def matmul(a, b):
    return jnp.dot(a, b, preferred_element_type=F32)


def shape(dims, kind=BF16):
    return jax.ShapeDtypeStruct(dims, kind)


def cost(flops, moved, transcendentals=0):
    return pl.CostEstimate(flops=flops, bytes_accessed=moved, transcendentals=transcendentals)


def params(mib):
    return pltpu.CompilerParams(vmem_limit_bytes=mib * MIB)


def packed_state(keys, base, values, low):
    columns = values.shape[1]
    first, last = low // HEAD, (low + columns - 1) // HEAD
    full = matmul(keys[first * HEAD - base : (last + 1) * HEAD - base, :], values)
    column = lax.broadcasted_iota(jnp.int32, (HEAD, columns), 1) + low
    total = jnp.zeros((HEAD, columns), F32)
    for h in range(first, last + 1):
        inside = (column >= h * HEAD) & (column < (h + 1) * HEAD)
        total = total + jnp.where(inside, full[(h - first) * HEAD : (h - first + 1) * HEAD, :], 0.0)
    return total


def split_state(core, state, mine_ref, send_ref):
    half = HEAD // 2
    mine_ref[...] = state[pl.ds(pl.multiple_of(core * half, 8), half), :]
    send_ref[...] = state[pl.ds(pl.multiple_of((1 - core) * half, 8), half), :].astype(BF16)


def first_kernel(
    core_ref, x_hbm, wk_hbm, wv_hbm, q_hbm, va_ref, keep_ref, mine_ref, send_ref, x_ref, wk_ref, wv_ref, q_ref,
    kt, state, tiles, row_sems, tile_sems, rest_sems
):
    count = x_ref.shape[0]
    parts = row_sems.shape[0]
    step = count // parts
    row_copies = [
        pltpu.make_async_copy(x_hbm.at[pl.ds(i * step, step), :], x_ref.at[pl.ds(i * step, step), :], row_sems.at[i])
        for i in range(parts)
    ]
    sources = [(wk_hbm, t) for t in range(3)] + [(wv_hbm, t) for t in range(2)]
    tile_copies = [
        pltpu.make_async_copy(source.at[:, pl.ds(t * TILE, TILE)], tiles.at[i], tile_sems.at[i])
        for i, (source, t) in enumerate(sources)
    ]
    inner = wk_hbm.shape[1]
    rest_copies = [
        pltpu.make_async_copy(wk_hbm.at[:, pl.ds(3 * TILE, inner - 3 * TILE)], wk_ref, rest_sems.at[0]),
        pltpu.make_async_copy(wv_hbm.at[:, pl.ds(FIRST, inner - FIRST)], wv_ref, rest_sems.at[1]),
        pltpu.make_async_copy(q_hbm, q_ref, rest_sems.at[2]),
    ]

    def keys(t, rows):
        kt[t * TILE : (t + 1) * TILE, rows] = feature_map(matmul(x_ref[rows, :], tiles[t])).astype(BF16).T

    def go(*cs):
        for c in cs:
            c.start()

    def end(*cs):
        for c in cs:
            c.wait()

    whole = slice(0, count)
    low, high = slice(0, step), slice(step, count)
    r, t5, rest = row_copies, tile_copies, rest_copies

    go(t5[0], t5[1], r[0], r[1])
    end(t5[0], t5[1], r[0])
    go(*t5[2:])
    keys(0, low)
    keys(1, low)
    end(r[1])
    go(*rest)
    keys(0, high)
    keys(1, high)
    end(*t5[2:])
    keys(2, whole)
    for t in range(2):
        va_ref[:, t * TILE : (t + 1) * TILE] = matmul(x_ref[...], tiles[3 + t]).astype(BF16)
    for t in range(2):
        low = t * TILE
        state[:, low : low + TILE] = packed_state(kt, 0, va_ref[:, low : low + TILE], low)
    keep_ref[...] = kt[FIRST // HEAD * HEAD : 3 * TILE, :]
    split_state(core_ref[0], state, mine_ref, send_ref)
    for copy in rest_copies:
        copy.wait()


HBM = pl.BlockSpec(memory_space=pltpu.HBM)


def first_part(core, flat, key_weight, value_weight, queries):
    count, model = flat.shape
    inner = key_weight.shape[1]
    half = HEAD // 2
    kept = 3 * TILE - FIRST // HEAD * HEAD
    return pl.pallas_call(
        first_kernel,
        in_specs=[SMEM] + [HBM] * 4,
        out_specs=[VMEM] * 8,
        scratch_shapes=[
            pltpu.VMEM((3 * TILE, count), BF16),
            pltpu.VMEM((HEAD, FIRST), F32),
            pltpu.VMEM((5, model, TILE), BF16),
            pltpu.SemaphoreType.DMA((2,)),
            pltpu.SemaphoreType.DMA((5,)),
            pltpu.SemaphoreType.DMA((3,)),
        ],
        out_shape=[
            shape((count, FIRST)),
            shape((kept, count)),
            shape((half, FIRST), F32),
            shape((half, FIRST)),
            shape((count, model)),
            shape((model, inner - 3 * TILE)),
            shape((model, inner - FIRST)),
            shape((count, inner)),
        ],
        compiler_params=params(18),
        cost_estimate=cost(10 * count * model * TILE, 2 * model * (count + 5 * TILE)),
        name="first_part",
    )(core, *(pltpu.with_memory_space_constraint(a, pltpu.HBM) for a in (flat, key_weight, value_weight, queries)))


def keys_kernel(order_ref, x_ref, wk_ref, k_ref):
    k_ref[...] = feature_map(matmul(x_ref[...], wk_ref[:, :TILE])).astype(BF16).T


def keys_part(order, flat, key_weight):
    count, model = flat.shape
    return pl.pallas_call(
        keys_kernel,
        in_specs=[SMEM, VMEM, VMEM],
        out_specs=VMEM,
        out_shape=shape((TILE, count)),
        compiler_params=params(6),
        cost_estimate=cost(2 * count * model * TILE, 2 * model * count),
        name="keys_part",
    )(order, flat, key_weight)


def pair_span(pair):
    start = 2 * HEAD * pair
    base = start // 128 * 128
    return base, start - base, 256 if start - base + 2 * HEAD <= 256 else 384


def paired(block, base, pair, limit):
    low, offset, wide = pair_span(pair)
    piece = block[:, low - base : min(low + wide, limit) - base]
    if piece.shape[1] < wide:
        piece = jnp.concatenate([piece, jnp.zeros((piece.shape[0], wide - piece.shape[1]), piece.dtype)], axis=1)
    if offset:
        piece = pltpu.roll(piece, wide - offset, 1)
    return piece[:, :256]


def mixed_kernel(order_ref, x_ref, wk_ref, wv_ref, k_ref, v_ref, both):
    rest = k_ref.shape[0]
    both[...] = jnp.zeros_like(both)
    both[:, :rest] = wk_ref[:, TILE:]
    both[:, 128 : 128 + rest] = wv_ref[:, 2 * TILE :]
    v_ref[:, :TILE] = matmul(x_ref[...], wv_ref[:, :TILE]).astype(BF16)
    out = matmul(x_ref[...], both[...])
    k_ref[...] = feature_map(out[:, :128]).astype(BF16).T[:rest, :]
    v_ref[:, TILE:] = out[:, 128 : 128 + rest].astype(BF16)


def mixed_part(order, flat, wk, wv):
    count, model = flat.shape
    rest = wk.shape[1] - TILE
    return pl.pallas_call(
        mixed_kernel,
        in_specs=[SMEM] + [VMEM] * 3,
        out_specs=[VMEM] * 2,
        out_shape=[shape((rest, count)), shape((count, TILE + rest))],
        scratch_shapes=[pltpu.VMEM((model, TILE), BF16)],
        compiler_params=params(10),
        cost_estimate=cost(4 * count * model * TILE, 2 * model * count),
        name="mixed_part",
    )(order, flat, wk, wv)


def last_kernel(core_ref, x_ref, wv_ref, ka_ref, kb_ref, kc_ref, va_ref, vb_ref, v_ref, mine_ref, send_ref, edge_ref, kt, state):
    width = edge_ref.shape[0]
    count = x_ref.shape[0]
    base = FIRST // HEAD * HEAD
    at = 0
    for part in (ka_ref, kb_ref, kc_ref):
        kt[at : at + part.shape[0], :] = part[...]
        at += part.shape[0]
    state[:, :TILE] = packed_state(kt, base, vb_ref[:, :TILE], FIRST)
    state[:, 2 * TILE :] = packed_state(kt, base, vb_ref[:, TILE:], 4 * TILE)
    v_ref[...] = matmul(x_ref[...], wv_ref[:, TILE : 2 * TILE]).astype(BF16)
    state[:, TILE : 2 * TILE] = packed_state(kt, base, v_ref[...], 3 * TILE)
    core = core_ref[0]
    split_state(core, state, mine_ref, send_ref)
    rows = pl.ds(pl.multiple_of((1 - core) * (count - width), 16), width)
    edge_ref[:, :FIRST] = va_ref[rows, :]
    edge_ref[:, FIRST : 3 * TILE] = vb_ref[rows, :TILE]
    edge_ref[:, 3 * TILE : 4 * TILE] = v_ref[rows, :]
    edge_ref[:, 4 * TILE :] = vb_ref[rows, TILE:]


def last_part(core, flat, value_weight, ka, kb, kc, va, vb, width):
    count, model = flat.shape
    inner = value_weight.shape[1] + FIRST
    half = HEAD // 2
    return pl.pallas_call(
        last_kernel,
        in_specs=[SMEM] + [VMEM] * 7,
        out_specs=[VMEM] * 4,
        out_shape=[
            shape((count, TILE)),
            shape((half, inner - FIRST), F32),
            shape((half, inner - FIRST)),
            shape((width, inner)),
        ],
        scratch_shapes=[
            pltpu.VMEM((inner - FIRST // HEAD * HEAD, count), BF16),
            pltpu.VMEM((HEAD, inner - FIRST), F32),
        ],
        compiler_params=params(10),
        cost_estimate=cost(3 * count * model * TILE, 2 * model * count),
        name="last_part",
    )(core, flat, value_weight, ka, kb, kc, va, vb)


def phi_kernel(order_ref, q_ref, qf_ref):
    inner = q_ref.shape[1]
    step = 160

    def rows(i, carry):
        here = pl.ds(pl.multiple_of(i * step, 16), step)
        for pair in range(inner // (2 * HEAD)):
            low, _, wide = pair_span(pair)
            q = q_ref[here, low : min(low + wide, inner)].astype(F32)
            q = feature_map(paired(q, low, pair, inner))
            qf_ref[here, pair * 256 : (pair + 1) * 256] = q.astype(BF16)
        return carry

    lax.fori_loop(0, q_ref.shape[0] // step, rows, 0)


def phi_queries(order, queries):
    count, inner = queries.shape
    pairs = inner // (2 * HEAD)
    return pl.pallas_call(
        phi_kernel,
        in_specs=[SMEM, VMEM],
        out_specs=VMEM,
        out_shape=shape((count, pairs * 256)),
        compiler_params=params(4),
        cost_estimate=cost(8 * count * inner, 4 * count * inner, count * inner),
        name="phi_queries",
    )(order, queries)


def row_branch(taps, w_ref, low, high):
    side = []
    for c in range(3):
        acc = taps[0] * w_ref[c : c + 1, low:high]
        acc = acc + taps[1] * w_ref[3 + c : 4 + c, low:high]
        side.append(acc + taps[2] * w_ref[6 + c : 7 + c, low:high])
    width = side[0].shape[0]
    place = lax.broadcasted_iota(jnp.int32, side[0].shape, 0)
    left = jnp.where(place > 0, pltpu.roll(side[0], 1, 0), 0.0)
    right = jnp.where(place < width - 1, pltpu.roll(side[2], width - 1, 0), 0.0)
    return side[1] + left + right


def lane_parts(va_ref, vb_ref, vc_ref, inner):
    for low in range(0, inner, 128):
        high = min(low + 128, inner)
        if low < FIRST:
            yield va_ref, low, low, high
        elif low < 3 * TILE:
            yield vb_ref, low - FIRST, low, high
        elif low < 4 * TILE:
            yield vc_ref, low - 3 * TILE, low, high
        else:
            yield vb_ref, low - 4 * TILE + TILE, low, high


def inner_rows(refs, w_ref, out_ref, width, first, number, at):
    va_ref, vb_ref, vc_ref = refs
    inner = out_ref.shape[1]

    def row(r, carry):
        here = pl.ds(pl.multiple_of((at + r) * width, 16), width)
        for ref, lane, low, high in lane_parts(va_ref, vb_ref, vc_ref, inner):
            taps = [
                ref[pl.ds(pl.multiple_of((first + r + d - 1) * width, 16), width), lane : lane + high - low].astype(F32)
                for d in range(3)
            ]
            out_ref[here, low:high] = row_branch(taps, w_ref, low, high)
        return carry

    lax.fori_loop(0, number, row, 0)


def middle_kernel(order_ref, va_ref, vb_ref, vc_ref, w_ref, out_ref, *, width):
    rows = va_ref.shape[0] // width
    inner_rows((va_ref, vb_ref, vc_ref), w_ref, out_ref, width, rows // 4, rows // 2, 0)


def border_kernel(core_ref, va_ref, vb_ref, vc_ref, halo_ref, w_ref, out_ref, *, width):
    rows = va_ref.shape[0] // width
    quarter = rows // 4
    refs = (va_ref, vb_ref, vc_ref)
    inner = out_ref.shape[1]
    inner_rows(refs, w_ref, out_ref, width, 1, quarter - 1, 1)
    inner_rows(refs, w_ref, out_ref, width, rows - quarter, quarter - 1, quarter)
    core = core_ref[0]
    top = (core == 1).astype(F32)
    bottom = (core == 0).astype(F32)
    last = (rows - 1) * width
    for ref, lane, low, high in lane_parts(*refs, inner):
        lanes = slice(lane, lane + high - low)
        halo = halo_ref[:, low:high].astype(F32)
        taps = [halo * top] + [ref[d * width : (d + 1) * width, lanes].astype(F32) for d in range(2)]
        out_ref[:width, low:high] = row_branch(taps, w_ref, low, high)
        taps = [ref[last + d * width : last + (d + 1) * width, lanes].astype(F32) for d in (-1, 0)] + [halo * bottom]
        end = (2 * quarter - 1) * width
        out_ref[end : end + width, low:high] = row_branch(taps, w_ref, low, high)


def local_rows(order, va, vb, vc, halo, conv_weight, width):
    count = va.shape[0]
    inner = conv_weight.shape[1]
    kernel = middle_kernel if halo is None else border_kernel
    operands = [va, vb, vc] + ([] if halo is None else [halo]) + [conv_weight]
    return pl.pallas_call(
        functools.partial(kernel, width=width),
        in_specs=[SMEM] + [VMEM] * len(operands),
        out_specs=VMEM,
        out_shape=shape((count // 2, inner), F32),
        compiler_params=params(4),
        cost_estimate=cost(10 * count * inner, 4 * count * inner),
        name="middle_rows" if halo is None else "border_rows",
    )(order, *operands)


def halves(core, own, other):
    own, other = own.astype(F32), other.astype(F32)
    return jnp.concatenate([jnp.where(core == 0, own, other), jnp.where(core == 0, other, own)], axis=0)


def pair_matrix(state, base, pair, limit):
    block = paired(state, base, pair, limit)
    column = lax.broadcasted_iota(jnp.int32, block.shape, 1)
    top = jnp.where(column < HEAD, block, 0.0)
    bottom = jnp.where((column >= HEAD) & (column < 2 * HEAD), block, 0.0)
    rest = jnp.zeros((256 - 2 * HEAD, 256), F32)
    return jnp.concatenate([top, bottom, rest], axis=0).astype(BF16)


def head_sums():
    row = lax.broadcasted_iota(jnp.int32, (256, 256), 0)
    column = lax.broadcasted_iota(jnp.int32, (256, 256), 1)
    first = (row < HEAD) & (column < HEAD)
    second = (row >= HEAD) & (row < 2 * HEAD) & (column >= HEAD) & (column < 2 * HEAD)
    return jnp.where(first | second, 1.0, 0.0).astype(BF16)


def normed_pair(qf, matrix, sums):
    attn = matmul(qf, matrix)
    total = matmul((attn * attn).astype(BF16), sums)
    return attn * lax.rsqrt(total * (1.0 / HEAD) + 1e-06)


def placed(normed, pairs, low, high):
    tiles = {}
    for pair, block in zip(pairs, normed):
        base, offset, wide = pair_span(pair)
        if wide > 256:
            block = jnp.concatenate([block, jnp.zeros((block.shape[0], wide - 256), F32)], axis=1)
        if offset:
            block = pltpu.roll(block, offset, 1)
        for t in range(wide // 128):
            at = base + t * 128
            piece = block[:, t * 128 : (t + 1) * 128]
            tiles[at] = tiles[at] + piece if at in tiles else piece
    for at in range(low, high, 128):
        yield at, min(at + 128, high), tiles[at][:, : min(128, high - at)]


CHUNK = 640


def early_kernel(core_ref, own_ref, other_ref, qf_ref, out_ref):
    state = halves(core_ref[0], own_ref[...], other_ref[...])
    sums = head_sums()
    pairs = range(FIRST // (2 * HEAD))
    matrices = [pair_matrix(state, 0, pair, FIRST) for pair in pairs]
    for at in range(0, qf_ref.shape[0], CHUNK):
        rows = slice(at, at + CHUNK)
        normed = [normed_pair(qf_ref[rows, pair * 256 : (pair + 1) * 256], matrices[pair], sums) for pair in pairs]
        for low, high, tile in placed(normed, pairs, 0, FIRST):
            out_ref[rows, low:high] = tile


def early_heads(core, own, other, qfeat):
    count = qfeat.shape[0]
    return pl.pallas_call(
        early_kernel,
        in_specs=[SMEM] + [VMEM] * 3,
        out_specs=VMEM,
        out_shape=shape((count, FIRST), F32),
        compiler_params=params(8),
        cost_estimate=cost(4 * count * FIRST * 512, 4 * count * FIRST),
        name="early_heads",
    )(core, own, other, qfeat)


def late_kernel(
    core_ref, owna_ref, othera_ref, ownb_ref, otherb_ref, qf_ref, mid_ref, edge_ref, early_ref, gain_ref, out_hbm,
    out, sems
):
    core = core_ref[0]
    count, inner = out_hbm.shape
    quarter = count // 4
    first = FIRST // (2 * HEAD)
    low = 2 * HEAD * first // 128 * 128
    state = jnp.concatenate(
        [halves(core, owna_ref[:, low:], othera_ref[:, low:]), halves(core, ownb_ref[...], otherb_ref[...])], axis=1
    )
    sums = head_sums()
    pairs = range(first, inner // (2 * HEAD))
    matrices = [pair_matrix(state, low, pair, inner) for pair in pairs]
    local = [edge_ref.at[:quarter], mid_ref.at[:quarter], mid_ref.at[quarter:], edge_ref.at[quarter:]]
    copies = []
    for at in range(0, count, CHUNK):
        rows = slice(at, at + CHUNK)
        normed = [
            normed_pair(qf_ref[rows, pair * 256 : (pair + 1) * 256], matrices[pair - first], sums) for pair in pairs
        ]
        later = {a: (b, tile) for a, b, tile in placed(normed, pairs, low, inner)}
        for part in range(at // quarter, (at + CHUNK) // quarter):
            here = slice(part * quarter, (part + 1) * quarter)
            inside = slice(part * quarter - at, (part + 1) * quarter - at)
            for a in range(0, inner, 128):
                b, tile = later.get(a, (a + 128, None))
                value = 0.0 if tile is None else tile[inside]
                if a < FIRST:
                    value = value + early_ref[here, a:b]
                out[here, a:b] = (value * gain_ref[:, a:b] + local[part][:, a:b]).astype(BF16)
            copies.append(pltpu.make_async_copy(out.at[here], out_hbm.at[here], sems.at[part]))
            copies[-1].start()
    for copy in copies:
        copy.wait()


def late_heads(core, first, second, qfeat, mid, edge, early, gain):
    count, inner = qfeat.shape[0], gain.shape[1]
    return pl.pallas_call(
        late_kernel,
        in_specs=[SMEM] + [VMEM] * 9,
        out_specs=HBM,
        scratch_shapes=[pltpu.VMEM((count, inner), BF16), pltpu.SemaphoreType.DMA((4,))],
        out_shape=shape((count, inner)),
        compiler_params=params(14),
        cost_estimate=cost(4 * count * inner * 512, 8 * count * inner),
        name="late_heads",
    )(core, *first, *second, qfeat, mid, edge, early, gain)


def swapped(block, axis, bit):
    return lax.ppermute(block, axis, [(i, i ^ bit) for i in range(lax.axis_size(axis))])


class Chain:
    def __init__(self, mine, send, masks):
        self.masks = list(masks)
        self.total = self.prefix = mine
        self.send = send
        self.received = None
        bits = [1 << b for b in range(len(self.masks))]
        self.rounds = [("space", 1)] + [("tm", bit) for bit in bits] + [("space", 0)]
        self.at = 0

    def done(self):
        return self.at == len(self.rounds)

    def left(self):
        return len(self.rounds) - self.at

    def start(self, send):
        axis, bit = self.rounds[self.at]
        self.send = send
        self.received = swapped(send, axis, bit or 1)

    def finish(self, received):
        axis, bit = self.rounds[self.at]
        self.at += 1
        self.received = None
        if bit == 0:
            self.result = (self.send, received)
            return
        received = received.astype(F32)
        if axis == "space":
            self.prefix = self.total + received
        else:
            self.prefix = self.prefix + self.masks.pop(0) * received
        self.total = self.total + received
        last = self.rounds[self.at][1] == 0
        self.send = (self.prefix if last else self.total).astype(BF16)


def shards(frames_in, queries, key_weight, value_weight, conv_weight, norm_gain):
    _, rows, width, model = frames_in.shape
    inner = key_weight.shape[1]
    count = rows * width
    core = lax.axis_index("space").astype(jnp.int32).reshape(1)
    flat = frames_in.reshape(count, model)
    gain = norm_gain.reshape(1, inner)
    frame = lax.axis_index("tm")
    masks = [(frame >> b & 1).astype(F32) for b in range((lax.axis_size("tm") - 1).bit_length())]
    core, masks = lax.optimization_barrier((core, masks))

    def slot(filler, starts=(), ends=(), extra=None):
        held, extra, order = lax.optimization_barrier((tuple(c.send for c in starts), extra, core))
        for c, send in zip(starts, held):
            c.start(send)
        moved = None if extra is None else swapped(extra, "space", 1)
        out = None if filler is None else filler(order)
        received, moved, out = lax.optimization_barrier((tuple(c.received for c in ends), moved, out))
        for c, r in zip(ends, received):
            c.finish(r)
        return out if extra is None else (out, moved)

    va, ka, mine, send, x, wk, wv, q = first_part(
        core, flat, key_weight, value_weight, queries.reshape(count, inner)
    )
    first = Chain(mine, send, masks)
    kb = slot(lambda order: keys_part(order, x, wk), [first], [first])
    kc, vb = slot(lambda order: mixed_part(order, x, wk, wv), [first], [first])
    vc, mine, send, edge = slot(
        lambda order: last_part(order, x, wv, ka, kb, kc, va, vb, width), [first], [first]
    )
    second = Chain(mine, send, masks)
    qfeat, halo = slot(lambda order: phi_queries(order, q), [second], [second], edge)
    fillers = [
        lambda order: local_rows(order, va, vb, vc, None, conv_weight, width),
        lambda order: local_rows(order, va, vb, vc, halo, conv_weight, width),
    ]
    local = []
    early = None
    while not second.done():
        filler = None
        if len(local) < 2:
            filler = fillers[len(local)]
        elif first.done() and early is None:
            filler = lambda order: early_heads(order, *first.result, qfeat)
        starts, ends = [second], [second]
        if not first.done():
            if first.received is None:
                starts = [second, first]
                if first.left() >= second.left() - 1:
                    ends = [second, first]
            else:
                ends = [second, first]
        out = slot(filler, starts, ends)
        if filler is not None and len(local) < 2:
            local.append(out)
        elif filler is not None:
            early = out
    mixed = late_heads(core, first.result, second.result, qfeat, *local, early, gain)
    return mixed.reshape(1, rows, width, inner)


def solution(mesh):
    in_specs = (
        P(("groups", "tm"), "space", None, None),
        P(("groups", "tm"), "space", None, None),
        P(),
        P(),
        P(),
        P(),
    )
    out_specs = P(("groups", "tm"), "space", None, None)
    return jax.shard_map(shards, mesh=mesh, in_specs=in_specs, out_specs=out_specs, check_vma=False)
```

```python
import functools

import jax
import jax.numpy as jnp
from jax import lax
from jax.experimental import pallas as pl
from jax.experimental.pallas import tpu as pltpu
from jax.sharding import PartitionSpec as P

HEAD = 112
TILE = 256
FIRST = 2 * TILE
F32 = jnp.float32
BF16 = jnp.bfloat16
MIB = 1 << 20
VMEM = pl.BlockSpec(memory_space=pltpu.VMEM)
SMEM = pl.BlockSpec(memory_space=pltpu.SMEM)


def feature_map(a):
    return jnp.maximum(a, 0.0) + jnp.exp(jnp.minimum(a, 0.0))


def matmul(a, b):
    return jnp.dot(a, b, preferred_element_type=F32)


def shape(dims, kind=BF16):
    return jax.ShapeDtypeStruct(dims, kind)


def cost(flops, moved, transcendentals=0):
    return pl.CostEstimate(flops=flops, bytes_accessed=moved, transcendentals=transcendentals)


def params(mib):
    return pltpu.CompilerParams(vmem_limit_bytes=mib * MIB)


def packed_state(keys, base, values, low):
    columns = values.shape[1]
    first, last = low // HEAD, (low + columns - 1) // HEAD
    full = matmul(keys[first * HEAD - base : (last + 1) * HEAD - base, :], values)
    column = lax.broadcasted_iota(jnp.int32, (HEAD, columns), 1) + low
    total = jnp.zeros((HEAD, columns), F32)
    for h in range(first, last + 1):
        inside = (column >= h * HEAD) & (column < (h + 1) * HEAD)
        total = total + jnp.where(inside, full[(h - first) * HEAD : (h - first + 1) * HEAD, :], 0.0)
    return total


def split_state(core, state, mine_ref, send_ref):
    half = HEAD // 2
    mine_ref[...] = state[pl.ds(pl.multiple_of(core * half, 8), half), :]
    send_ref[...] = state[pl.ds(pl.multiple_of((1 - core) * half, 8), half), :].astype(BF16)


def project_kernel(
    core_ref, x_hbm, wk_hbm, wv_hbm, q_hbm, v_ref, mine_ref, send_ref, edge_ref, q_ref,
    x_ref, tiles, ends, both, kt, state, row_sems, tile_sems, rest_sems
):
    count, inner = v_ref.shape
    width = edge_ref.shape[0]
    full = inner // TILE
    rest = inner - full * TILE
    step = count // 2
    low, high, whole = slice(0, step), slice(step, count), slice(0, count)
    rows = [
        pltpu.make_async_copy(x_hbm.at[pl.ds(i * step, step), :], x_ref.at[pl.ds(i * step, step), :], row_sems.at[i])
        for i in range(2)
    ]
    sources = [(wk_hbm, t) for t in range(full)] + [(wv_hbm, t) for t in range(full)]
    copies = [
        pltpu.make_async_copy(source.at[:, pl.ds(t * TILE, TILE)], tiles.at[i], tile_sems.at[i])
        for i, (source, t) in enumerate(sources)
    ]
    copies += [
        pltpu.make_async_copy(source.at[:, pl.ds(full * TILE, rest)], ends.at[i], rest_sems.at[i])
        for i, source in enumerate((wk_hbm, wv_hbm))
    ]
    query_copy = pltpu.make_async_copy(q_hbm, q_ref, rest_sems.at[2])

    def keys(t, here):
        kt[t * TILE : (t + 1) * TILE, here] = feature_map(matmul(x_ref[here, :], tiles[t])).astype(BF16).T

    def values(t):
        v_ref[:, t * TILE : (t + 1) * TILE] = matmul(x_ref[...], tiles[full + t]).astype(BF16)

    def states(t):
        at = slice(t * TILE, min((t + 1) * TILE, inner))
        state[:, at] = packed_state(kt, 0, v_ref[:, at], t * TILE)

    for copy in (copies[0], copies[1], *rows):
        copy.start()
    for copy in (copies[0], copies[1], rows[0]):
        copy.wait()
    for copy in copies[2:]:
        copy.start()
    keys(0, low)
    keys(1, low)
    rows[1].wait()
    query_copy.start()
    keys(0, high)
    keys(1, high)
    for copy in copies[2:]:
        copy.wait()
    both[...] = jnp.zeros_like(both)
    both[:, :rest] = ends[0]
    both[:, 128 : 128 + rest] = ends[1]
    for t in range(2, full):
        keys(t, whole)
    out = matmul(x_ref[...], both[...])
    kt[full * TILE :, :] = feature_map(out[:, :128]).astype(BF16).T[:rest, :]
    v_ref[:, full * TILE :] = out[:, 128 : 128 + rest].astype(BF16)
    for t in range(full):
        values(t)
    for t in range(full + 1):
        states(t)
    core = core_ref[0]
    split_state(core, state, mine_ref, send_ref)
    edge_ref[...] = v_ref[pl.ds(pl.multiple_of((1 - core) * (count - width), 16), width), :]
    query_copy.wait()


HBM = pl.BlockSpec(memory_space=pltpu.HBM)


def project(core, flat, key_weight, value_weight, queries, width):
    count, model = flat.shape
    inner = key_weight.shape[1]
    half = HEAD // 2
    full = inner // TILE
    return pl.pallas_call(
        project_kernel,
        in_specs=[SMEM] + [HBM] * 4,
        out_specs=[VMEM] * 5,
        scratch_shapes=[
            pltpu.VMEM((count, model), BF16),
            pltpu.VMEM((2 * full, model, TILE), BF16),
            pltpu.VMEM((2, model, inner - full * TILE), BF16),
            pltpu.VMEM((model, TILE), BF16),
            pltpu.VMEM((inner, count), BF16),
            pltpu.VMEM((HEAD, inner), F32),
            pltpu.SemaphoreType.DMA((2,)),
            pltpu.SemaphoreType.DMA((2 * full,)),
            pltpu.SemaphoreType.DMA((3,)),
        ],
        out_shape=[
            shape((count, inner)),
            shape((half, inner), F32),
            shape((half, inner)),
            shape((width, inner)),
            shape((count, inner)),
        ],
        compiler_params=params(30),
        cost_estimate=cost(4 * count * model * inner, 2 * model * (count + 2 * inner)),
        name="project",
    )(core, *(pltpu.with_memory_space_constraint(a, pltpu.HBM) for a in (flat, key_weight, value_weight, queries)))


def pair_span(pair):
    start = 2 * HEAD * pair
    base = start // 128 * 128
    return base, start - base, 256 if start - base + 2 * HEAD <= 256 else 384


def paired(block, base, pair, limit):
    low, offset, wide = pair_span(pair)
    piece = block[:, low - base : min(low + wide, limit) - base]
    if piece.shape[1] < wide:
        piece = jnp.concatenate([piece, jnp.zeros((piece.shape[0], wide - piece.shape[1]), piece.dtype)], axis=1)
    if offset:
        piece = pltpu.roll(piece, wide - offset, 1)
    return piece[:, :256]


def phi_kernel(order_ref, q_ref, qf_ref):
    inner = q_ref.shape[1]
    step = 160

    def rows(i, carry):
        here = pl.ds(pl.multiple_of(i * step, 16), step)
        for pair in range(inner // (2 * HEAD)):
            low, _, wide = pair_span(pair)
            q = q_ref[here, low : min(low + wide, inner)].astype(F32)
            q = feature_map(paired(q, low, pair, inner))
            qf_ref[here, pair * 256 : (pair + 1) * 256] = q.astype(BF16)
        return carry

    lax.fori_loop(0, q_ref.shape[0] // step, rows, 0)


def phi_queries(order, queries):
    count, inner = queries.shape
    pairs = inner // (2 * HEAD)
    return pl.pallas_call(
        phi_kernel,
        in_specs=[SMEM, VMEM],
        out_specs=VMEM,
        out_shape=shape((count, pairs * 256)),
        compiler_params=params(4),
        cost_estimate=cost(8 * count * inner, 4 * count * inner, count * inner),
        name="phi_queries",
    )(order, queries)


def row_branch(taps, w_ref, low, high):
    side = []
    for c in range(3):
        acc = taps[0] * w_ref[c : c + 1, low:high]
        acc = acc + taps[1] * w_ref[3 + c : 4 + c, low:high]
        side.append(acc + taps[2] * w_ref[6 + c : 7 + c, low:high])
    width = side[0].shape[0]
    place = lax.broadcasted_iota(jnp.int32, side[0].shape, 0)
    left = jnp.where(place > 0, pltpu.roll(side[0], 1, 0), 0.0)
    right = jnp.where(place < width - 1, pltpu.roll(side[2], width - 1, 0), 0.0)
    return side[1] + left + right


def lane_tiles(inner):
    return [(low, min(low + 128, inner)) for low in range(0, inner, 128)]


def inner_rows(v_ref, w_ref, out_ref, width, first, number, at):

    def row(r, carry):
        here = pl.ds(pl.multiple_of((at + r) * width, 16), width)
        for low, high in lane_tiles(out_ref.shape[1]):
            taps = [
                v_ref[pl.ds(pl.multiple_of((first + r + d - 1) * width, 16), width), low:high].astype(F32)
                for d in range(3)
            ]
            out_ref[here, low:high] = row_branch(taps, w_ref, low, high)
        return carry

    lax.fori_loop(0, number, row, 0)


def middle_kernel(order_ref, v_ref, w_ref, out_ref, *, width):
    rows = v_ref.shape[0] // width
    inner_rows(v_ref, w_ref, out_ref, width, rows // 4, rows // 2, 0)


def border_kernel(core_ref, v_ref, halo_ref, w_ref, out_ref, *, width):
    rows = v_ref.shape[0] // width
    quarter = rows // 4
    inner_rows(v_ref, w_ref, out_ref, width, 1, quarter - 1, 1)
    inner_rows(v_ref, w_ref, out_ref, width, rows - quarter, quarter - 1, quarter)
    core = core_ref[0]
    top = (core == 1).astype(F32)
    bottom = (core == 0).astype(F32)
    last = (rows - 1) * width
    for low, high in lane_tiles(out_ref.shape[1]):
        halo = halo_ref[:, low:high].astype(F32)
        taps = [halo * top] + [v_ref[d * width : (d + 1) * width, low:high].astype(F32) for d in range(2)]
        out_ref[:width, low:high] = row_branch(taps, w_ref, low, high)
        taps = [v_ref[last + d * width : last + (d + 1) * width, low:high].astype(F32) for d in (-1, 0)] + [halo * bottom]
        end = (2 * quarter - 1) * width
        out_ref[end : end + width, low:high] = row_branch(taps, w_ref, low, high)


def local_rows(order, values, halo, conv_weight, width):
    count, inner = values.shape
    kernel = middle_kernel if halo is None else border_kernel
    operands = [values] + ([] if halo is None else [halo]) + [conv_weight]
    return pl.pallas_call(
        functools.partial(kernel, width=width),
        in_specs=[SMEM] + [VMEM] * len(operands),
        out_specs=VMEM,
        out_shape=shape((count // 2, inner), F32),
        compiler_params=params(4),
        cost_estimate=cost(10 * count * inner, 4 * count * inner),
        name="middle_rows" if halo is None else "border_rows",
    )(order, *operands)


def halves(core, own, other):
    own, other = own.astype(F32), other.astype(F32)
    return jnp.concatenate([jnp.where(core == 0, own, other), jnp.where(core == 0, other, own)], axis=0)


def pair_matrix(state, base, pair, limit):
    block = paired(state, base, pair, limit)
    column = lax.broadcasted_iota(jnp.int32, block.shape, 1)
    top = jnp.where(column < HEAD, block, 0.0)
    bottom = jnp.where((column >= HEAD) & (column < 2 * HEAD), block, 0.0)
    rest = jnp.zeros((256 - 2 * HEAD, 256), F32)
    return jnp.concatenate([top, bottom, rest], axis=0).astype(BF16)


def head_sums():
    row = lax.broadcasted_iota(jnp.int32, (256, 256), 0)
    column = lax.broadcasted_iota(jnp.int32, (256, 256), 1)
    first = (row < HEAD) & (column < HEAD)
    second = (row >= HEAD) & (row < 2 * HEAD) & (column >= HEAD) & (column < 2 * HEAD)
    return jnp.where(first | second, 1.0, 0.0).astype(BF16)


def normed_pair(qf, matrix, sums):
    attn = matmul(qf, matrix)
    total = matmul((attn * attn).astype(BF16), sums)
    return attn * lax.rsqrt(total * (1.0 / HEAD) + 1e-06)


def placed(normed, pairs, low, high):
    tiles = {}
    for pair, block in zip(pairs, normed):
        base, offset, wide = pair_span(pair)
        if wide > 256:
            block = jnp.concatenate([block, jnp.zeros((block.shape[0], wide - 256), F32)], axis=1)
        if offset:
            block = pltpu.roll(block, offset, 1)
        for t in range(wide // 128):
            at = base + t * 128
            piece = block[:, t * 128 : (t + 1) * 128]
            tiles[at] = tiles[at] + piece if at in tiles else piece
    for at in range(low, high, 128):
        yield at, min(at + 128, high), tiles[at][:, : min(128, high - at)]


CHUNK = 640


def early_kernel(core_ref, own_ref, other_ref, qf_ref, out_ref):
    state = halves(core_ref[0], own_ref[...], other_ref[...])
    sums = head_sums()
    pairs = range(FIRST // (2 * HEAD))
    matrices = [pair_matrix(state, 0, pair, FIRST) for pair in pairs]
    for at in range(0, qf_ref.shape[0], CHUNK):
        rows = slice(at, at + CHUNK)
        normed = [normed_pair(qf_ref[rows, pair * 256 : (pair + 1) * 256], matrices[pair], sums) for pair in pairs]
        for low, high, tile in placed(normed, pairs, 0, FIRST):
            out_ref[rows, low:high] = tile


def early_heads(core, own, other, qfeat):
    count = qfeat.shape[0]
    return pl.pallas_call(
        early_kernel,
        in_specs=[SMEM] + [VMEM] * 3,
        out_specs=VMEM,
        out_shape=shape((count, FIRST), F32),
        compiler_params=params(8),
        cost_estimate=cost(4 * count * FIRST * 512, 4 * count * FIRST),
        name="early_heads",
    )(core, own, other, qfeat)


def late_kernel(
    core_ref, owna_ref, othera_ref, ownb_ref, otherb_ref, qf_ref, mid_ref, edge_ref, early_ref, gain_ref, out_hbm,
    out, sems
):
    core = core_ref[0]
    count, inner = out_hbm.shape
    quarter = count // 4
    first = FIRST // (2 * HEAD)
    low = 2 * HEAD * first // 128 * 128
    state = jnp.concatenate(
        [halves(core, owna_ref[:, low:], othera_ref[:, low:]), halves(core, ownb_ref[...], otherb_ref[...])], axis=1
    )
    sums = head_sums()
    pairs = range(first, inner // (2 * HEAD))
    matrices = [pair_matrix(state, low, pair, inner) for pair in pairs]
    local = [edge_ref.at[:quarter], mid_ref.at[:quarter], mid_ref.at[quarter:], edge_ref.at[quarter:]]
    copies = []
    for at in range(0, count, CHUNK):
        rows = slice(at, at + CHUNK)
        normed = [
            normed_pair(qf_ref[rows, pair * 256 : (pair + 1) * 256], matrices[pair - first], sums) for pair in pairs
        ]
        later = {a: (b, tile) for a, b, tile in placed(normed, pairs, low, inner)}
        for part in range(at // quarter, (at + CHUNK) // quarter):
            here = slice(part * quarter, (part + 1) * quarter)
            inside = slice(part * quarter - at, (part + 1) * quarter - at)
            for a in range(0, inner, 128):
                b, tile = later.get(a, (a + 128, None))
                value = 0.0 if tile is None else tile[inside]
                if a < FIRST:
                    value = value + early_ref[here, a:b]
                out[here, a:b] = (value * gain_ref[:, a:b] + local[part][:, a:b]).astype(BF16)
            copies.append(pltpu.make_async_copy(out.at[here], out_hbm.at[here], sems.at[part]))
            copies[-1].start()
    for copy in copies:
        copy.wait()


def late_heads(core, first, second, qfeat, mid, edge, early, gain):
    count, inner = qfeat.shape[0], gain.shape[1]
    return pl.pallas_call(
        late_kernel,
        in_specs=[SMEM] + [VMEM] * 9,
        out_specs=HBM,
        scratch_shapes=[pltpu.VMEM((count, inner), BF16), pltpu.SemaphoreType.DMA((4,))],
        out_shape=shape((count, inner)),
        compiler_params=params(14),
        cost_estimate=cost(4 * count * inner * 512, 8 * count * inner),
        name="late_heads",
    )(core, *first, *second, qfeat, mid, edge, early, gain)


def swapped(block, axis, bit):
    return lax.ppermute(block, axis, [(i, i ^ bit) for i in range(lax.axis_size(axis))])


def shards(frames_in, queries, key_weight, value_weight, conv_weight, norm_gain):
    _, rows, width, model = frames_in.shape
    inner = key_weight.shape[1]
    count = rows * width
    core = lax.axis_index("space").astype(jnp.int32).reshape(1)
    flat = frames_in.reshape(count, model)
    gain = norm_gain.reshape(1, inner)
    frame = lax.axis_index("tm")
    masks = [(frame >> b & 1).astype(F32) for b in range((lax.axis_size("tm") - 1).bit_length())]
    core, masks = lax.optimization_barrier((core, masks))

    def slot(filler, sends):
        arrays, order = lax.optimization_barrier((tuple(a for a, _, _ in sends), core))
        received = tuple(swapped(a, axis, bit) for a, (_, axis, bit) in zip(arrays, sends))
        out = None if filler is None else filler(order)
        return lax.optimization_barrier((received, out))

    values, mine, send, edge, q = project(
        core, flat, key_weight, value_weight, queries.reshape(count, inner), width
    )
    (other, halo), _ = slot(None, [(send, "space", 1), (edge, "space", 1)])
    total = prefix = mine + other.astype(F32)
    local, qfeat = [], None
    for b, mask in enumerate(masks):
        left = len(masks) - 1 - b
        filler = None
        if left == 0:
            filler = lambda order: phi_queries(order, q)
        elif left == 1:
            filler = lambda order: local_rows(order, values, halo, conv_weight, width)
        elif left == 2:
            filler = lambda order: local_rows(order, values, None, conv_weight, width)
        (other,), out = slot(filler, [(total.astype(BF16), "tm", 1 << b)])
        if left == 0:
            qfeat = out
        elif filler is not None:
            local.append(out)
        other = other.astype(F32)
        prefix = prefix + mask * other
        total = total + other
    prefix = prefix.astype(BF16)
    parts = prefix[:, :FIRST], prefix[:, FIRST:]
    parts = lax.optimization_barrier(parts)
    others = [swapped(part, "space", 1) for part in parts]
    early = early_heads(core, parts[0], others[0], qfeat)
    others[1], early = lax.optimization_barrier((others[1], early))
    mixed = late_heads(core, (parts[0], others[0]), (parts[1], others[1]), qfeat, *local, early, gain)
    return mixed.reshape(1, rows, width, inner)


def solution(mesh):
    in_specs = (
        P(("groups", "tm"), "space", None, None),
        P(("groups", "tm"), "space", None, None),
        P(),
        P(),
        P(),
        P(),
    )
    out_specs = P(("groups", "tm"), "space", None, None)
    return jax.shard_map(shards, mesh=mesh, in_specs=in_specs, out_specs=out_specs, check_vma=False)
```

```python
import functools

import jax
import jax.numpy as jnp
from jax import lax
from jax.experimental import pallas as pl
from jax.experimental.pallas import tpu as pltpu
from jax.sharding import PartitionSpec as P

HEAD = 112
TILE = 256
FIRST = 2 * TILE
F32 = jnp.float32
BF16 = jnp.bfloat16
MIB = 1 << 20
VMEM = pl.BlockSpec(memory_space=pltpu.VMEM)
SMEM = pl.BlockSpec(memory_space=pltpu.SMEM)


def feature_map(a):
    return jnp.maximum(a, 0.0) + jnp.exp(jnp.minimum(a, 0.0))


def matmul(a, b):
    return jnp.dot(a, b, preferred_element_type=F32)


def shape(dims, kind=BF16):
    return jax.ShapeDtypeStruct(dims, kind)


def cost(flops, moved, transcendentals=0):
    return pl.CostEstimate(flops=flops, bytes_accessed=moved, transcendentals=transcendentals)


def params(mib):
    return pltpu.CompilerParams(vmem_limit_bytes=mib * MIB)


def packed_state(keys, base, values, low):
    columns = values.shape[1]
    first, last = low // HEAD, (low + columns - 1) // HEAD
    full = matmul(keys[first * HEAD - base : (last + 1) * HEAD - base, :], values)
    column = lax.broadcasted_iota(jnp.int32, (HEAD, columns), 1) + low
    total = jnp.zeros((HEAD, columns), F32)
    for h in range(first, last + 1):
        inside = (column >= h * HEAD) & (column < (h + 1) * HEAD)
        total = total + jnp.where(inside, full[(h - first) * HEAD : (h - first + 1) * HEAD, :], 0.0)
    return total


def split_state(core, state, mine_ref, send_ref):
    half = HEAD // 2
    mine_ref[...] = state[pl.ds(pl.multiple_of(core * half, 8), half), :]
    send_ref[...] = state[pl.ds(pl.multiple_of((1 - core) * half, 8), half), :].astype(BF16)


def project_kernel(
    core_ref, x_hbm, wk_hbm, wv_hbm, q_hbm, v_ref, mine_ref, send_ref, edge_ref, q_ref,
    x_ref, tiles, ends, both, kt, state, row_sems, tile_sems, rest_sems
):
    count, inner = v_ref.shape
    width = edge_ref.shape[0]
    full = inner // TILE
    rest = inner - full * TILE
    step = count // 2
    low, high, whole = slice(0, step), slice(step, count), slice(0, count)
    rows = [
        pltpu.make_async_copy(x_hbm.at[pl.ds(i * step, step), :], x_ref.at[pl.ds(i * step, step), :], row_sems.at[i])
        for i in range(2)
    ]
    sources = [(wk_hbm, t) for t in range(full)] + [(wv_hbm, t) for t in range(full)]
    copies = [
        pltpu.make_async_copy(source.at[:, pl.ds(t * TILE, TILE)], tiles.at[i], tile_sems.at[i])
        for i, (source, t) in enumerate(sources)
    ]
    copies += [
        pltpu.make_async_copy(source.at[:, pl.ds(full * TILE, rest)], ends.at[i], rest_sems.at[i])
        for i, source in enumerate((wk_hbm, wv_hbm))
    ]
    query_copy = pltpu.make_async_copy(q_hbm, q_ref, rest_sems.at[2])

    def keys(t, here):
        kt[t * TILE : (t + 1) * TILE, here] = feature_map(matmul(x_ref[here, :], tiles[t])).astype(BF16).T

    def values(t):
        v_ref[:, t * TILE : (t + 1) * TILE] = matmul(x_ref[...], tiles[full + t]).astype(BF16)

    def states(t):
        at = slice(t * TILE, min((t + 1) * TILE, inner))
        state[:, at] = packed_state(kt, 0, v_ref[:, at], t * TILE)

    for copy in (copies[0], copies[1], *rows):
        copy.start()
    for copy in (copies[0], copies[1], rows[0]):
        copy.wait()
    for copy in copies[2:]:
        copy.start()
    keys(0, low)
    keys(1, low)
    rows[1].wait()
    query_copy.start()
    keys(0, high)
    keys(1, high)
    for copy in copies[2:]:
        copy.wait()
    both[...] = jnp.zeros_like(both)
    both[:, :rest] = ends[0]
    both[:, 128 : 128 + rest] = ends[1]
    for t in range(2, full):
        keys(t, whole)
    out = matmul(x_ref[...], both[...])
    kt[full * TILE :, :] = feature_map(out[:, :128]).astype(BF16).T[:rest, :]
    v_ref[:, full * TILE :] = out[:, 128 : 128 + rest].astype(BF16)
    for t in range(full):
        values(t)
    for t in range(full + 1):
        states(t)
    core = core_ref[0]
    split_state(core, state, mine_ref, send_ref)
    edge_ref[...] = v_ref[pl.ds(pl.multiple_of((1 - core) * (count - width), 16), width), :]
    query_copy.wait()


HBM = pl.BlockSpec(memory_space=pltpu.HBM)


def project(core, flat, key_weight, value_weight, queries, width):
    count, model = flat.shape
    inner = key_weight.shape[1]
    half = HEAD // 2
    full = inner // TILE
    return pl.pallas_call(
        project_kernel,
        in_specs=[SMEM] + [HBM] * 4,
        out_specs=[VMEM] * 5,
        scratch_shapes=[
            pltpu.VMEM((count, model), BF16),
            pltpu.VMEM((2 * full, model, TILE), BF16),
            pltpu.VMEM((2, model, inner - full * TILE), BF16),
            pltpu.VMEM((model, TILE), BF16),
            pltpu.VMEM((inner, count), BF16),
            pltpu.VMEM((HEAD, inner), F32),
            pltpu.SemaphoreType.DMA((2,)),
            pltpu.SemaphoreType.DMA((2 * full,)),
            pltpu.SemaphoreType.DMA((3,)),
        ],
        out_shape=[
            shape((count, inner)),
            shape((half, inner), F32),
            shape((half, inner)),
            shape((width, inner)),
            shape((count, inner)),
        ],
        compiler_params=params(30),
        cost_estimate=cost(4 * count * model * inner, 2 * model * (count + 2 * inner)),
        name="project",
    )(core, *(pltpu.with_memory_space_constraint(a, pltpu.HBM) for a in (flat, key_weight, value_weight, queries)))


def pair_span(pair):
    start = 2 * HEAD * pair
    base = start // 128 * 128
    return base, start - base, 256 if start - base + 2 * HEAD <= 256 else 384


def paired(block, base, pair, limit):
    low, offset, wide = pair_span(pair)
    piece = block[:, low - base : min(low + wide, limit) - base]
    if piece.shape[1] < wide:
        piece = jnp.concatenate([piece, jnp.zeros((piece.shape[0], wide - piece.shape[1]), piece.dtype)], axis=1)
    if offset:
        piece = pltpu.roll(piece, wide - offset, 1)
    return piece[:, :256]


def phi_kernel(order_ref, q_ref, qf_ref):
    inner = q_ref.shape[1]
    step = 160

    def rows(i, carry):
        here = pl.ds(pl.multiple_of(i * step, 16), step)
        for pair in range(inner // (2 * HEAD)):
            low, _, wide = pair_span(pair)
            q = q_ref[here, low : min(low + wide, inner)].astype(F32)
            q = feature_map(paired(q, low, pair, inner))
            qf_ref[here, pair * 256 : (pair + 1) * 256] = q.astype(BF16)
        return carry

    lax.fori_loop(0, q_ref.shape[0] // step, rows, 0)


def phi_queries(order, queries):
    count, inner = queries.shape
    pairs = inner // (2 * HEAD)
    return pl.pallas_call(
        phi_kernel,
        in_specs=[SMEM, VMEM],
        out_specs=VMEM,
        out_shape=shape((count, pairs * 256)),
        compiler_params=params(4),
        cost_estimate=cost(8 * count * inner, 4 * count * inner, count * inner),
        name="phi_queries",
    )(order, queries)


def row_branch(taps, w_ref, low, high):
    side = []
    for c in range(3):
        acc = taps[0] * w_ref[c : c + 1, low:high]
        acc = acc + taps[1] * w_ref[3 + c : 4 + c, low:high]
        side.append(acc + taps[2] * w_ref[6 + c : 7 + c, low:high])
    width = side[0].shape[0]
    place = lax.broadcasted_iota(jnp.int32, side[0].shape, 0)
    left = jnp.where(place > 0, pltpu.roll(side[0], 1, 0), 0.0)
    right = jnp.where(place < width - 1, pltpu.roll(side[2], width - 1, 0), 0.0)
    return side[1] + left + right


def lane_tiles(inner):
    return [(low, min(low + 128, inner)) for low in range(0, inner, 128)]


def inner_rows(v_ref, w_ref, out_ref, width, first, number, at):

    def row(r, carry):
        here = pl.ds(pl.multiple_of((at + r) * width, 16), width)
        for low, high in lane_tiles(out_ref.shape[1]):
            taps = [
                v_ref[pl.ds(pl.multiple_of((first + r + d - 1) * width, 16), width), low:high].astype(F32)
                for d in range(3)
            ]
            out_ref[here, low:high] = row_branch(taps, w_ref, low, high)
        return carry

    lax.fori_loop(0, number, row, 0)


def middle_kernel(order_ref, v_ref, w_ref, out_ref, *, width):
    rows = v_ref.shape[0] // width
    inner_rows(v_ref, w_ref, out_ref, width, rows // 4, rows // 2, 0)


def border_kernel(core_ref, v_ref, halo_ref, w_ref, out_ref, *, width):
    rows = v_ref.shape[0] // width
    quarter = rows // 4
    inner_rows(v_ref, w_ref, out_ref, width, 1, quarter - 1, 1)
    inner_rows(v_ref, w_ref, out_ref, width, rows - quarter, quarter - 1, quarter)
    core = core_ref[0]
    top = (core == 1).astype(F32)
    bottom = (core == 0).astype(F32)
    last = (rows - 1) * width
    for low, high in lane_tiles(out_ref.shape[1]):
        halo = halo_ref[:, low:high].astype(F32)
        taps = [halo * top] + [v_ref[d * width : (d + 1) * width, low:high].astype(F32) for d in range(2)]
        out_ref[:width, low:high] = row_branch(taps, w_ref, low, high)
        taps = [v_ref[last + d * width : last + (d + 1) * width, low:high].astype(F32) for d in (-1, 0)] + [halo * bottom]
        end = (2 * quarter - 1) * width
        out_ref[end : end + width, low:high] = row_branch(taps, w_ref, low, high)


def local_rows(order, values, halo, conv_weight, width):
    count, inner = values.shape
    kernel = middle_kernel if halo is None else border_kernel
    operands = [values] + ([] if halo is None else [halo]) + [conv_weight]
    return pl.pallas_call(
        functools.partial(kernel, width=width),
        in_specs=[SMEM] + [VMEM] * len(operands),
        out_specs=VMEM,
        out_shape=shape((count // 2, inner), F32),
        compiler_params=params(4),
        cost_estimate=cost(10 * count * inner, 4 * count * inner),
        name="middle_rows" if halo is None else "border_rows",
    )(order, *operands)


def halves(core, own, other):
    own, other = own.astype(F32), other.astype(F32)
    return jnp.concatenate([jnp.where(core == 0, own, other), jnp.where(core == 0, other, own)], axis=0)


def pair_matrix(state, base, pair, limit):
    block = paired(state, base, pair, limit)
    column = lax.broadcasted_iota(jnp.int32, block.shape, 1)
    top = jnp.where(column < HEAD, block, 0.0)
    bottom = jnp.where((column >= HEAD) & (column < 2 * HEAD), block, 0.0)
    rest = jnp.zeros((256 - 2 * HEAD, 256), F32)
    return jnp.concatenate([top, bottom, rest], axis=0).astype(BF16)


def head_sums():
    row = lax.broadcasted_iota(jnp.int32, (256, 256), 0)
    column = lax.broadcasted_iota(jnp.int32, (256, 256), 1)
    first = (row < HEAD) & (column < HEAD)
    second = (row >= HEAD) & (row < 2 * HEAD) & (column >= HEAD) & (column < 2 * HEAD)
    return jnp.where(first | second, 1.0, 0.0).astype(BF16)


def normed_pair(qf, matrix, sums):
    attn = matmul(qf, matrix)
    total = matmul((attn * attn).astype(BF16), sums)
    return attn * lax.rsqrt(total * (1.0 / HEAD) + 1e-06)


def placed(normed, pairs, low, high):
    tiles = {}
    for pair, block in zip(pairs, normed):
        base, offset, wide = pair_span(pair)
        if wide > 256:
            block = jnp.concatenate([block, jnp.zeros((block.shape[0], wide - 256), F32)], axis=1)
        if offset:
            block = pltpu.roll(block, offset, 1)
        for t in range(wide // 128):
            at = base + t * 128
            piece = block[:, t * 128 : (t + 1) * 128]
            tiles[at] = tiles[at] + piece if at in tiles else piece
    for at in range(low, high, 128):
        yield at, min(at + 128, high), tiles[at][:, : min(128, high - at)]


CHUNK = 640


def early_kernel(core_ref, own_ref, other_ref, qf_ref, out_ref):
    state = halves(core_ref[0], own_ref[...], other_ref[...])
    sums = head_sums()
    pairs = range(FIRST // (2 * HEAD))
    matrices = [pair_matrix(state, 0, pair, FIRST) for pair in pairs]
    for at in range(0, qf_ref.shape[0], CHUNK):
        rows = slice(at, at + CHUNK)
        normed = [normed_pair(qf_ref[rows, pair * 256 : (pair + 1) * 256], matrices[pair], sums) for pair in pairs]
        for low, high, tile in placed(normed, pairs, 0, FIRST):
            out_ref[rows, low:high] = tile


def early_heads(core, own, other, qfeat):
    count = qfeat.shape[0]
    return pl.pallas_call(
        early_kernel,
        in_specs=[SMEM] + [VMEM] * 3,
        out_specs=VMEM,
        out_shape=shape((count, FIRST), F32),
        compiler_params=params(8),
        cost_estimate=cost(4 * count * FIRST * 512, 4 * count * FIRST),
        name="early_heads",
    )(core, own, other, qfeat)


def late_kernel(
    core_ref, owna_ref, othera_ref, ownb_ref, otherb_ref, qf_ref, mid_ref, edge_ref, early_ref, gain_ref, out_hbm,
    out, sems
):
    core = core_ref[0]
    count, inner = out_hbm.shape
    quarter = count // 4
    first = FIRST // (2 * HEAD)
    low = 2 * HEAD * first // 128 * 128
    state = jnp.concatenate(
        [halves(core, owna_ref[:, low:], othera_ref[:, low:]), halves(core, ownb_ref[...], otherb_ref[...])], axis=1
    )
    sums = head_sums()
    pairs = range(first, inner // (2 * HEAD))
    matrices = [pair_matrix(state, low, pair, inner) for pair in pairs]
    local = [edge_ref.at[:quarter], mid_ref.at[:quarter], mid_ref.at[quarter:], edge_ref.at[quarter:]]
    copies = []
    for at in range(0, count, CHUNK):
        rows = slice(at, at + CHUNK)
        normed = [
            normed_pair(qf_ref[rows, pair * 256 : (pair + 1) * 256], matrices[pair - first], sums) for pair in pairs
        ]
        later = {a: (b, tile) for a, b, tile in placed(normed, pairs, low, inner)}
        for part in range(at // quarter, (at + CHUNK) // quarter):
            here = slice(part * quarter, (part + 1) * quarter)
            inside = slice(part * quarter - at, (part + 1) * quarter - at)
            for a in range(0, inner, 128):
                b, tile = later.get(a, (a + 128, None))
                value = 0.0 if tile is None else tile[inside]
                if a < FIRST:
                    value = value + early_ref[here, a:b]
                out[here, a:b] = (value * gain_ref[:, a:b] + local[part][:, a:b]).astype(BF16)
            copies.append(pltpu.make_async_copy(out.at[here], out_hbm.at[here], sems.at[part]))
            copies[-1].start()
    for copy in copies:
        copy.wait()


def late_heads(core, first, second, qfeat, mid, edge, early, gain):
    count, inner = qfeat.shape[0], gain.shape[1]
    return pl.pallas_call(
        late_kernel,
        in_specs=[SMEM] + [VMEM] * 9,
        out_specs=HBM,
        scratch_shapes=[pltpu.VMEM((count, inner), BF16), pltpu.SemaphoreType.DMA((4,))],
        out_shape=shape((count, inner)),
        compiler_params=params(14),
        cost_estimate=cost(4 * count * inner * 512, 8 * count * inner),
        name="late_heads",
    )(core, *first, *second, qfeat, mid, edge, early, gain)


def swapped(block, axis, bit):
    return lax.ppermute(block, axis, [(i, i ^ bit) for i in range(lax.axis_size(axis))])


def shards(frames_in, queries, key_weight, value_weight, conv_weight, norm_gain):
    _, rows, width, model = frames_in.shape
    inner = key_weight.shape[1]
    count = rows * width
    core = lax.axis_index("space").astype(jnp.int32).reshape(1)
    flat = frames_in.reshape(count, model)
    gain = norm_gain.reshape(1, inner)
    frame = lax.axis_index("tm")
    masks = [(frame >> b & 1).astype(F32) for b in range((lax.axis_size("tm") - 1).bit_length())]
    core, masks = lax.optimization_barrier((core, masks))

    values, mine, send, edge, q = project(
        core, flat, key_weight, value_weight, queries.reshape(count, inner), width
    )
    cuts = [slice(0, FIRST), slice(FIRST, inner)]
    sends = [send[:, cut] for cut in cuts]
    received = [swapped(part, "space", 1) for part in sends]
    halo = swapped(edge, "space", 1)
    totals = [mine[:, cut] + other.astype(F32) for cut, other in zip(cuts, received)]
    prefixes = list(totals)
    local, qfeat = [], None
    for b, mask in enumerate(masks):
        left = len(masks) - 1 - b
        filler = None
        if left == 0:
            filler = lambda order: phi_queries(order, q)
        elif left == 1:
            filler = lambda order: local_rows(order, values, halo, conv_weight, width)
        elif left == 2:
            filler = lambda order: local_rows(order, values, None, conv_weight, width)
        outs = [total.astype(BF16) for total in totals]
        outs[1], order = lax.optimization_barrier((outs[1], core))
        received = [swapped(out, "tm", 1 << b) for out in outs]
        if filler is not None:
            out = filler(order)
            received[0], out = lax.optimization_barrier((received[0], out))
            if left == 0:
                qfeat = out
            else:
                local.append(out)
        for i, other in enumerate(received):
            other = other.astype(F32)
            prefixes[i] = prefixes[i] + mask * other
            totals[i] = totals[i] + other
    parts = [prefix.astype(BF16) for prefix in prefixes]
    others = [swapped(part, "space", 1) for part in parts]
    early = early_heads(core, parts[0], others[0], qfeat)
    others[1], early = lax.optimization_barrier((others[1], early))
    mixed = late_heads(core, (parts[0], others[0]), (parts[1], others[1]), qfeat, *local, early, gain)
    return mixed.reshape(1, rows, width, inner)


def solution(mesh):
    in_specs = (
        P(("groups", "tm"), "space", None, None),
        P(("groups", "tm"), "space", None, None),
        P(),
        P(),
        P(),
        P(),
    )
    out_specs = P(("groups", "tm"), "space", None, None)
    return jax.shard_map(shards, mesh=mesh, in_specs=in_specs, out_specs=out_specs, check_vma=False)
```

```python
import functools

import jax
import jax.numpy as jnp
from jax import lax
from jax.experimental import pallas as pl
from jax.experimental.pallas import tpu as pltpu
from jax.sharding import PartitionSpec as P

HEAD = 112
TILE = 256
FIRST = 2 * TILE
F32 = jnp.float32
BF16 = jnp.bfloat16
MIB = 1 << 20
VMEM = pl.BlockSpec(memory_space=pltpu.VMEM)
SMEM = pl.BlockSpec(memory_space=pltpu.SMEM)


def feature_map(a):
    return jnp.maximum(a, 0.0) + jnp.exp(jnp.minimum(a, 0.0))


def matmul(a, b):
    return jnp.dot(a, b, preferred_element_type=F32)


def shape(dims, kind=BF16):
    return jax.ShapeDtypeStruct(dims, kind)


def cost(flops, moved, transcendentals=0):
    return pl.CostEstimate(flops=flops, bytes_accessed=moved, transcendentals=transcendentals)


def params(mib):
    return pltpu.CompilerParams(vmem_limit_bytes=mib * MIB)


def packed_state(keys, base, values, low):
    columns = values.shape[1]
    first, last = low // HEAD, (low + columns - 1) // HEAD
    full = matmul(keys[first * HEAD - base : (last + 1) * HEAD - base, :], values)
    column = lax.broadcasted_iota(jnp.int32, (HEAD, columns), 1) + low
    total = jnp.zeros((HEAD, columns), F32)
    for h in range(first, last + 1):
        inside = (column >= h * HEAD) & (column < (h + 1) * HEAD)
        total = total + jnp.where(inside, full[(h - first) * HEAD : (h - first + 1) * HEAD, :], 0.0)
    return total


def split_state(core, state, mine_ref, send_ref):
    half = HEAD // 2
    mine_ref[...] = state[pl.ds(pl.multiple_of(core * half, 8), half), :]
    send_ref[...] = state[pl.ds(pl.multiple_of((1 - core) * half, 8), half), :].astype(BF16)


def project_kernel(
    core_ref, x_hbm, wk_hbm, wv_hbm, q_hbm, v_ref, mine_ref, send_ref, edge_ref, q_ref,
    x_ref, tiles, ends, both, kt, state, row_sems, tile_sems, rest_sems
):
    count, inner = v_ref.shape
    width = edge_ref.shape[0]
    full = inner // TILE
    rest = inner - full * TILE
    step = count // 2
    low, high, whole = slice(0, step), slice(step, count), slice(0, count)
    rows = [
        pltpu.make_async_copy(x_hbm.at[pl.ds(i * step, step), :], x_ref.at[pl.ds(i * step, step), :], row_sems.at[i])
        for i in range(2)
    ]
    sources = [(wk_hbm, t) for t in range(full)] + [(wv_hbm, t) for t in range(full)]
    copies = [
        pltpu.make_async_copy(source.at[:, pl.ds(t * TILE, TILE)], tiles.at[i], tile_sems.at[i])
        for i, (source, t) in enumerate(sources)
    ]
    copies += [
        pltpu.make_async_copy(source.at[:, pl.ds(full * TILE, rest)], ends.at[i], rest_sems.at[i])
        for i, source in enumerate((wk_hbm, wv_hbm))
    ]
    query_copy = pltpu.make_async_copy(q_hbm, q_ref, rest_sems.at[2])

    def keys(t, here):
        kt[t * TILE : (t + 1) * TILE, here] = feature_map(matmul(x_ref[here, :], tiles[t])).astype(BF16).T

    def values(t):
        v_ref[:, t * TILE : (t + 1) * TILE] = matmul(x_ref[...], tiles[full + t]).astype(BF16)

    def states(t):
        at = slice(t * TILE, min((t + 1) * TILE, inner))
        state[:, at] = packed_state(kt, 0, v_ref[:, at], t * TILE)

    for copy in (copies[0], copies[1], *rows):
        copy.start()
    for copy in (copies[0], copies[1], rows[0]):
        copy.wait()
    for copy in copies[2:]:
        copy.start()
    keys(0, low)
    keys(1, low)
    rows[1].wait()
    query_copy.start()
    keys(0, high)
    keys(1, high)
    for copy in copies[2:]:
        copy.wait()
    both[...] = jnp.zeros_like(both)
    both[:, :rest] = ends[0]
    both[:, 128 : 128 + rest] = ends[1]
    for t in range(2, full):
        keys(t, whole)
    out = matmul(x_ref[...], both[...])
    kt[full * TILE :, :] = feature_map(out[:, :128]).astype(BF16).T[:rest, :]
    v_ref[:, full * TILE :] = out[:, 128 : 128 + rest].astype(BF16)
    for t in range(full):
        values(t)
    for t in range(full + 1):
        states(t)
    core = core_ref[0]
    split_state(core, state, mine_ref, send_ref)
    edge_ref[...] = v_ref[pl.ds(pl.multiple_of((1 - core) * (count - width), 16), width), :]
    query_copy.wait()


HBM = pl.BlockSpec(memory_space=pltpu.HBM)


def project(core, flat, key_weight, value_weight, queries, width):
    count, model = flat.shape
    inner = key_weight.shape[1]
    half = HEAD // 2
    full = inner // TILE
    return pl.pallas_call(
        project_kernel,
        in_specs=[SMEM] + [HBM] * 4,
        out_specs=[VMEM] * 5,
        scratch_shapes=[
            pltpu.VMEM((count, model), BF16),
            pltpu.VMEM((2 * full, model, TILE), BF16),
            pltpu.VMEM((2, model, inner - full * TILE), BF16),
            pltpu.VMEM((model, TILE), BF16),
            pltpu.VMEM((inner, count), BF16),
            pltpu.VMEM((HEAD, inner), F32),
            pltpu.SemaphoreType.DMA((2,)),
            pltpu.SemaphoreType.DMA((2 * full,)),
            pltpu.SemaphoreType.DMA((3,)),
        ],
        out_shape=[
            shape((count, inner)),
            shape((half, inner), F32),
            shape((half, inner)),
            shape((width, inner)),
            shape((count, inner)),
        ],
        compiler_params=params(30),
        cost_estimate=cost(4 * count * model * inner, 2 * model * (count + 2 * inner)),
        name="project",
    )(core, *(pltpu.with_memory_space_constraint(a, pltpu.HBM) for a in (flat, key_weight, value_weight, queries)))


def pair_span(pair):
    start = 2 * HEAD * pair
    base = start // 128 * 128
    return base, start - base, 256 if start - base + 2 * HEAD <= 256 else 384


def paired(block, base, pair, limit):
    low, offset, wide = pair_span(pair)
    piece = block[:, low - base : min(low + wide, limit) - base]
    if piece.shape[1] < wide:
        piece = jnp.concatenate([piece, jnp.zeros((piece.shape[0], wide - piece.shape[1]), piece.dtype)], axis=1)
    if offset:
        piece = pltpu.roll(piece, wide - offset, 1)
    return piece[:, :256]


def phi_kernel(order_ref, q_ref, qf_ref):
    inner = q_ref.shape[1]
    step = 160

    def rows(i, carry):
        here = pl.ds(pl.multiple_of(i * step, 16), step)
        for pair in range(inner // (2 * HEAD)):
            low, _, wide = pair_span(pair)
            q = q_ref[here, low : min(low + wide, inner)].astype(F32)
            q = feature_map(paired(q, low, pair, inner))
            qf_ref[here, pair * 256 : (pair + 1) * 256] = q.astype(BF16)
        return carry

    lax.fori_loop(0, q_ref.shape[0] // step, rows, 0)


def phi_queries(order, queries):
    count, inner = queries.shape
    pairs = inner // (2 * HEAD)
    return pl.pallas_call(
        phi_kernel,
        in_specs=[SMEM, VMEM],
        out_specs=VMEM,
        out_shape=shape((count, pairs * 256)),
        compiler_params=params(4),
        cost_estimate=cost(8 * count * inner, 4 * count * inner, count * inner),
        name="phi_queries",
    )(order, queries)


def row_branch(taps, w_ref, low, high):
    side = []
    for c in range(3):
        acc = taps[0] * w_ref[c : c + 1, low:high]
        acc = acc + taps[1] * w_ref[3 + c : 4 + c, low:high]
        side.append(acc + taps[2] * w_ref[6 + c : 7 + c, low:high])
    width = side[0].shape[0]
    place = lax.broadcasted_iota(jnp.int32, side[0].shape, 0)
    left = jnp.where(place > 0, pltpu.roll(side[0], 1, 0), 0.0)
    right = jnp.where(place < width - 1, pltpu.roll(side[2], width - 1, 0), 0.0)
    return side[1] + left + right


def lane_tiles(inner):
    return [(low, min(low + 128, inner)) for low in range(0, inner, 128)]


def inner_rows(v_ref, w_ref, out_ref, width, first, number, at):

    def row(r, carry):
        here = pl.ds(pl.multiple_of((at + r) * width, 16), width)
        for low, high in lane_tiles(out_ref.shape[1]):
            taps = [
                v_ref[pl.ds(pl.multiple_of((first + r + d - 1) * width, 16), width), low:high].astype(F32)
                for d in range(3)
            ]
            out_ref[here, low:high] = row_branch(taps, w_ref, low, high)
        return carry

    lax.fori_loop(0, number, row, 0)


def middle_kernel(order_ref, v_ref, w_ref, out_ref, *, width, first):
    inner_rows(v_ref, w_ref, out_ref, width, first, out_ref.shape[0] // width, 0)


def border_kernel(core_ref, v_ref, halo_ref, w_ref, out_ref, *, width, top, bottom):
    rows = v_ref.shape[0] // width
    inner_rows(v_ref, w_ref, out_ref, width, 1, top - 1, 1)
    inner_rows(v_ref, w_ref, out_ref, width, rows - bottom, bottom - 1, top)
    core = core_ref[0]
    above = (core == 1).astype(F32)
    below = (core == 0).astype(F32)
    last = (rows - 1) * width
    for low, high in lane_tiles(out_ref.shape[1]):
        halo = halo_ref[:, low:high].astype(F32)
        taps = [halo * above] + [v_ref[d * width : (d + 1) * width, low:high].astype(F32) for d in range(2)]
        out_ref[:width, low:high] = row_branch(taps, w_ref, low, high)
        taps = [v_ref[last + d * width : last + (d + 1) * width, low:high].astype(F32) for d in (-1, 0)]
        end = (top + bottom - 1) * width
        out_ref[end : end + width, low:high] = row_branch(taps + [halo * below], w_ref, low, high)


def local_rows(kernel, number, name, order, *operands):
    width, inner = kernel.keywords["width"], operands[0].shape[1]
    return pl.pallas_call(
        kernel,
        in_specs=[SMEM] + [VMEM] * len(operands),
        out_specs=VMEM,
        out_shape=shape((number * width, inner), F32),
        compiler_params=params(4),
        cost_estimate=cost(20 * number * width * inner, 8 * number * width * inner),
        name=name,
    )(order, *operands)


def row_pieces(rows):
    top, bottom = rows // 4, 2
    upper = (rows - top - bottom) // 2
    return top, bottom, upper, rows - top - bottom - upper


def halves(core, own, other):
    own, other = own.astype(F32), other.astype(F32)
    return jnp.concatenate([jnp.where(core == 0, own, other), jnp.where(core == 0, other, own)], axis=0)


def pair_matrix(state, base, pair, limit):
    block = paired(state, base, pair, limit)
    column = lax.broadcasted_iota(jnp.int32, block.shape, 1)
    top = jnp.where(column < HEAD, block, 0.0)
    bottom = jnp.where((column >= HEAD) & (column < 2 * HEAD), block, 0.0)
    rest = jnp.zeros((256 - 2 * HEAD, 256), F32)
    return jnp.concatenate([top, bottom, rest], axis=0).astype(BF16)


def head_sums():
    row = lax.broadcasted_iota(jnp.int32, (256, 256), 0)
    column = lax.broadcasted_iota(jnp.int32, (256, 256), 1)
    first = (row < HEAD) & (column < HEAD)
    second = (row >= HEAD) & (row < 2 * HEAD) & (column >= HEAD) & (column < 2 * HEAD)
    return jnp.where(first | second, 1.0, 0.0).astype(BF16)


def normed_pair(qf, matrix, sums):
    attn = matmul(qf, matrix)
    total = matmul((attn * attn).astype(BF16), sums)
    return attn * lax.rsqrt(total * (1.0 / HEAD) + 1e-06)


def placed(normed, pairs, low, high):
    tiles = {}
    for pair, block in zip(pairs, normed):
        base, offset, wide = pair_span(pair)
        if wide > 256:
            block = jnp.concatenate([block, jnp.zeros((block.shape[0], wide - 256), F32)], axis=1)
        if offset:
            block = pltpu.roll(block, offset, 1)
        for t in range(wide // 128):
            at = base + t * 128
            piece = block[:, t * 128 : (t + 1) * 128]
            tiles[at] = tiles[at] + piece if at in tiles else piece
    for at in range(low, high, 128):
        yield at, min(at + 128, high), tiles[at][:, : min(128, high - at)]


CHUNK = 640


def early_kernel(core_ref, own_ref, other_ref, qf_ref, out_ref):
    state = halves(core_ref[0], own_ref[...], other_ref[...])
    sums = head_sums()
    pairs = range(FIRST // (2 * HEAD))
    matrices = [pair_matrix(state, 0, pair, FIRST) for pair in pairs]
    for at in range(0, qf_ref.shape[0], CHUNK):
        rows = slice(at, at + CHUNK)
        normed = [normed_pair(qf_ref[rows, pair * 256 : (pair + 1) * 256], matrices[pair], sums) for pair in pairs]
        for low, high, tile in placed(normed, pairs, 0, FIRST):
            out_ref[rows, low:high] = tile


def early_heads(core, own, other, qfeat):
    count = qfeat.shape[0]
    return pl.pallas_call(
        early_kernel,
        in_specs=[SMEM] + [VMEM] * 3,
        out_specs=VMEM,
        out_shape=shape((count, FIRST), F32),
        compiler_params=params(8),
        cost_estimate=cost(4 * count * FIRST * 512, 4 * count * FIRST),
        name="early_heads",
    )(core, own, other, qfeat)


def late_kernel(
    core_ref, owna_ref, othera_ref, ownb_ref, otherb_ref, qf_ref, upper_ref, lower_ref, edge_ref, early_ref,
    gain_ref, out_hbm, out, sems, *, width
):
    core = core_ref[0]
    count, inner = out_hbm.shape
    first = FIRST // (2 * HEAD)
    low = 2 * HEAD * first // 128 * 128
    state = jnp.concatenate(
        [halves(core, owna_ref[:, low:], othera_ref[:, low:]), halves(core, ownb_ref[...], otherb_ref[...])], axis=1
    )
    sums = head_sums()
    pairs = range(first, inner // (2 * HEAD))
    matrices = [pair_matrix(state, low, pair, inner) for pair in pairs]
    top, bottom, upper, lower = (n * width for n in row_pieces(count // width))
    pieces = [
        (0, top, edge_ref, 0),
        (top, upper, upper_ref, 0),
        (top + upper, lower, lower_ref, 0),
        (count - bottom, bottom, edge_ref, top),
    ]
    copies = []
    for at in range(0, count, CHUNK):
        rows = slice(at, at + CHUNK)
        normed = [
            normed_pair(qf_ref[rows, pair * 256 : (pair + 1) * 256], matrices[pair - first], sums) for pair in pairs
        ]
        later = {a: (b, tile) for a, b, tile in placed(normed, pairs, low, inner)}
        for start, number, ref, base in pieces:
            lo, hi = max(start, at), min(start + number, at + CHUNK)
            if lo >= hi:
                continue
            here = slice(lo, hi)
            inside = slice(lo - at, hi - at)
            there = slice(lo - start + base, hi - start + base)
            for a in range(0, inner, 128):
                b, tile = later.get(a, (a + 128, None))
                value = 0.0 if tile is None else tile[inside]
                if a < FIRST:
                    value = value + early_ref[here, a:b]
                out[here, a:b] = (value * gain_ref[:, a:b] + ref[there, a:b]).astype(BF16)
            copies.append(pltpu.make_async_copy(out.at[here], out_hbm.at[here], sems.at[len(copies)]))
            copies[-1].start()
    for copy in copies:
        copy.wait()


def late_heads(core, first, second, qfeat, local, early, gain, width):
    count, inner = qfeat.shape[0], gain.shape[1]
    return pl.pallas_call(
        functools.partial(late_kernel, width=width),
        in_specs=[SMEM] + [VMEM] * 10,
        out_specs=HBM,
        scratch_shapes=[pltpu.VMEM((count, inner), BF16), pltpu.SemaphoreType.DMA((8,))],
        out_shape=shape((count, inner)),
        compiler_params=params(14),
        cost_estimate=cost(4 * count * inner * 512, 8 * count * inner),
        name="late_heads",
    )(core, *first, *second, qfeat, *local, early, gain)


def swapped(block, axis, bit):
    return lax.ppermute(block, axis, [(i, i ^ bit) for i in range(lax.axis_size(axis))])


def shards(frames_in, queries, key_weight, value_weight, conv_weight, norm_gain):
    _, rows, width, model = frames_in.shape
    inner = key_weight.shape[1]
    count = rows * width
    core = lax.axis_index("space").astype(jnp.int32).reshape(1)
    flat = frames_in.reshape(count, model)
    gain = norm_gain.reshape(1, inner)
    frame = lax.axis_index("tm")
    masks = [(frame >> b & 1).astype(F32) for b in range((lax.axis_size("tm") - 1).bit_length())]
    core, masks = lax.optimization_barrier((core, masks))

    values, mine, send, edge, q = project(
        core, flat, key_weight, value_weight, queries.reshape(count, inner), width
    )
    cuts = [slice(0, FIRST), slice(FIRST, inner)]
    sends = [send[:, cut] for cut in cuts]
    received = [swapped(part, "space", 1) for part in sends]
    halo = swapped(edge, "space", 1)
    totals = [mine[:, cut] + other.astype(F32) for cut, other in zip(cuts, received)]
    prefixes = list(totals)
    top, bottom, upper, lower = row_pieces(rows)
    middle = lambda first: functools.partial(middle_kernel, width=width, first=first)
    border = functools.partial(border_kernel, width=width, top=top, bottom=bottom)
    kernels = {
        2: lambda order: local_rows(middle(top), upper, "upper_rows", order, values, conv_weight),
        1: lambda order: local_rows(middle(top + upper), lower, "lower_rows", order, values, conv_weight),
        0: lambda order: (
            phi_queries(order, q),
            local_rows(border, top + bottom, "border_rows", order, values, halo, conv_weight),
        ),
    }
    local, qfeat = [], None
    for b, mask in enumerate(masks):
        left = len(masks) - 1 - b
        filler = kernels.get(left)
        outs = [total.astype(BF16) for total in totals]
        outs[1], order = lax.optimization_barrier((outs[1], core))
        received = [swapped(out, "tm", 1 << b) for out in outs]
        if filler is not None:
            out = filler(order)
            received[0], out = lax.optimization_barrier((received[0], out))
            if left == 0:
                qfeat, out = out
            local.append(out)
        for i, other in enumerate(received):
            other = other.astype(F32)
            prefixes[i] = prefixes[i] + mask * other
            totals[i] = totals[i] + other
    parts = [prefix.astype(BF16) for prefix in prefixes]
    others = [swapped(part, "space", 1) for part in parts]
    early = early_heads(core, parts[0], others[0], qfeat)
    others[1], early = lax.optimization_barrier((others[1], early))
    mixed = late_heads(core, (parts[0], others[0]), (parts[1], others[1]), qfeat, local, early, gain, width)
    return mixed.reshape(1, rows, width, inner)


def solution(mesh):
    in_specs = (
        P(("groups", "tm"), "space", None, None),
        P(("groups", "tm"), "space", None, None),
        P(),
        P(),
        P(),
        P(),
    )
    out_specs = P(("groups", "tm"), "space", None, None)
    return jax.shard_map(shards, mesh=mesh, in_specs=in_specs, out_specs=out_specs, check_vma=False)
```

```python
import functools

import jax
import jax.numpy as jnp
from jax import lax
from jax.experimental import pallas as pl
from jax.experimental.pallas import tpu as pltpu
from jax.sharding import PartitionSpec as P

HEAD = 112
TILE = 256
FIRST = 2 * TILE
F32 = jnp.float32
BF16 = jnp.bfloat16
MIB = 1 << 20
VMEM = pl.BlockSpec(memory_space=pltpu.VMEM)
SMEM = pl.BlockSpec(memory_space=pltpu.SMEM)


def feature_map(a):
    return jnp.maximum(a, 0.0) + jnp.exp(jnp.minimum(a, 0.0))


def matmul(a, b):
    return jnp.dot(a, b, preferred_element_type=F32)


def shape(dims, kind=BF16):
    return jax.ShapeDtypeStruct(dims, kind)


def cost(flops, moved, transcendentals=0):
    return pl.CostEstimate(flops=flops, bytes_accessed=moved, transcendentals=transcendentals)


def params(mib):
    return pltpu.CompilerParams(vmem_limit_bytes=mib * MIB)


def packed_state(keys, base, values, low):
    columns = values.shape[1]
    first, last = low // HEAD, (low + columns - 1) // HEAD
    full = matmul(keys[first * HEAD - base : (last + 1) * HEAD - base, :], values)
    column = lax.broadcasted_iota(jnp.int32, (HEAD, columns), 1) + low
    total = jnp.zeros((HEAD, columns), F32)
    for h in range(first, last + 1):
        inside = (column >= h * HEAD) & (column < (h + 1) * HEAD)
        total = total + jnp.where(inside, full[(h - first) * HEAD : (h - first + 1) * HEAD, :], 0.0)
    return total


def split_state(core, state, mine_ref, send_ref):
    half = HEAD // 2
    mine_ref[...] = state[pl.ds(pl.multiple_of(core * half, 8), half), :]
    send_ref[...] = state[pl.ds(pl.multiple_of((1 - core) * half, 8), half), :].astype(BF16)


def project_kernel(
    core_ref, x_hbm, wk_hbm, wv_hbm, q_hbm, v_ref, mine_ref, send_ref, edge_ref, q_ref,
    x_ref, tiles, ends, both, kt, state, row_sems, tile_sems, rest_sems
):
    count, inner = v_ref.shape
    width = edge_ref.shape[0]
    full = inner // TILE
    rest = inner - full * TILE
    step = count // 2
    low, high, whole = slice(0, step), slice(step, count), slice(0, count)
    rows = [
        pltpu.make_async_copy(x_hbm.at[pl.ds(i * step, step), :], x_ref.at[pl.ds(i * step, step), :], row_sems.at[i])
        for i in range(2)
    ]
    sources = [(wk_hbm, t) for t in range(full)] + [(wv_hbm, t) for t in range(full)]
    copies = [
        pltpu.make_async_copy(source.at[:, pl.ds(t * TILE, TILE)], tiles.at[i], tile_sems.at[i])
        for i, (source, t) in enumerate(sources)
    ]
    copies += [
        pltpu.make_async_copy(source.at[:, pl.ds(full * TILE, rest)], ends.at[i], rest_sems.at[i])
        for i, source in enumerate((wk_hbm, wv_hbm))
    ]
    query_copy = pltpu.make_async_copy(q_hbm, q_ref, rest_sems.at[2])

    def keys(t, here):
        kt[t * TILE : (t + 1) * TILE, here] = feature_map(matmul(x_ref[here, :], tiles[t])).astype(BF16).T

    def values(t):
        v_ref[:, t * TILE : (t + 1) * TILE] = matmul(x_ref[...], tiles[full + t]).astype(BF16)

    def states(t):
        at = slice(t * TILE, min((t + 1) * TILE, inner))
        state[:, at] = packed_state(kt, 0, v_ref[:, at], t * TILE)

    for copy in (copies[0], copies[1], *rows):
        copy.start()
    for copy in (copies[0], copies[1], rows[0]):
        copy.wait()
    for copy in copies[2:]:
        copy.start()
    keys(0, low)
    keys(1, low)
    rows[1].wait()
    query_copy.start()
    keys(0, high)
    keys(1, high)
    for copy in copies[2:]:
        copy.wait()
    both[...] = jnp.zeros_like(both)
    both[:, :rest] = ends[0]
    both[:, 128 : 128 + rest] = ends[1]
    for t in range(2, full):
        keys(t, whole)
    out = matmul(x_ref[...], both[...])
    kt[full * TILE :, :] = feature_map(out[:, :128]).astype(BF16).T[:rest, :]
    v_ref[:, full * TILE :] = out[:, 128 : 128 + rest].astype(BF16)
    for t in range(full):
        values(t)
    for t in range(full + 1):
        states(t)
    core = core_ref[0]
    split_state(core, state, mine_ref, send_ref)
    edge_ref[...] = v_ref[pl.ds(pl.multiple_of((1 - core) * (count - width), 16), width), :]
    query_copy.wait()


HBM = pl.BlockSpec(memory_space=pltpu.HBM)


def project(core, flat, key_weight, value_weight, queries, width):
    count, model = flat.shape
    inner = key_weight.shape[1]
    half = HEAD // 2
    full = inner // TILE
    return pl.pallas_call(
        project_kernel,
        in_specs=[SMEM] + [HBM] * 4,
        out_specs=[VMEM] * 5,
        scratch_shapes=[
            pltpu.VMEM((count, model), BF16),
            pltpu.VMEM((2 * full, model, TILE), BF16),
            pltpu.VMEM((2, model, inner - full * TILE), BF16),
            pltpu.VMEM((model, TILE), BF16),
            pltpu.VMEM((inner, count), BF16),
            pltpu.VMEM((HEAD, inner), F32),
            pltpu.SemaphoreType.DMA((2,)),
            pltpu.SemaphoreType.DMA((2 * full,)),
            pltpu.SemaphoreType.DMA((3,)),
        ],
        out_shape=[
            shape((count, inner)),
            shape((half, inner), F32),
            shape((half, inner)),
            shape((width, inner)),
            shape((count, inner)),
        ],
        compiler_params=params(30),
        cost_estimate=cost(4 * count * model * inner, 2 * model * (count + 2 * inner)),
        name="project",
    )(core, *(pltpu.with_memory_space_constraint(a, pltpu.HBM) for a in (flat, key_weight, value_weight, queries)))


def pair_span(pair):
    start = 2 * HEAD * pair
    base = start // 128 * 128
    return base, start - base, 256 if start - base + 2 * HEAD <= 256 else 384


def paired(block, base, pair, limit):
    low, offset, wide = pair_span(pair)
    piece = block[:, low - base : min(low + wide, limit) - base]
    if piece.shape[1] < wide:
        piece = jnp.concatenate([piece, jnp.zeros((piece.shape[0], wide - piece.shape[1]), piece.dtype)], axis=1)
    if offset:
        piece = pltpu.roll(piece, wide - offset, 1)
    return piece[:, :256]


def phi_kernel(order_ref, q_ref, qf_ref):
    inner = q_ref.shape[1]
    step = 160

    def rows(i, carry):
        here = pl.ds(pl.multiple_of(i * step, 16), step)
        for pair in range(inner // (2 * HEAD)):
            low, _, wide = pair_span(pair)
            q = feature_map(q_ref[here, low : min(low + wide, inner)].astype(F32)).astype(BF16)
            qf_ref[here, pair * 256 : (pair + 1) * 256] = paired(q, low, pair, inner)
        return carry

    lax.fori_loop(0, q_ref.shape[0] // step, rows, 0)


def phi_queries(order, queries):
    count, inner = queries.shape
    pairs = inner // (2 * HEAD)
    return pl.pallas_call(
        phi_kernel,
        in_specs=[SMEM, VMEM],
        out_specs=VMEM,
        out_shape=shape((count, pairs * 256)),
        compiler_params=params(4),
        cost_estimate=cost(8 * count * inner, 4 * count * inner, count * inner),
        name="phi_queries",
    )(order, queries)


def row_branch(taps, w_ref, low, high):
    side = []
    for c in range(3):
        acc = taps[0] * w_ref[c : c + 1, low:high]
        acc = acc + taps[1] * w_ref[3 + c : 4 + c, low:high]
        side.append(acc + taps[2] * w_ref[6 + c : 7 + c, low:high])
    width = side[0].shape[0]
    place = lax.broadcasted_iota(jnp.int32, side[0].shape, 0)
    left = jnp.where(place > 0, pltpu.roll(side[0], 1, 0), 0.0)
    right = jnp.where(place < width - 1, pltpu.roll(side[2], width - 1, 0), 0.0)
    return side[1] + left + right


def lane_tiles(inner):
    return [(low, min(low + 128, inner)) for low in range(0, inner, 128)]


def inner_rows(v_ref, w_ref, out_ref, width, first, number, at):

    def row(r, carry):
        here = pl.ds(pl.multiple_of((at + r) * width, 16), width)
        for low, high in lane_tiles(out_ref.shape[1]):
            taps = [
                v_ref[pl.ds(pl.multiple_of((first + r + d - 1) * width, 16), width), low:high].astype(F32)
                for d in range(3)
            ]
            out_ref[here, low:high] = row_branch(taps, w_ref, low, high)
        return carry

    lax.fori_loop(0, number, row, 0)


def middle_kernel(order_ref, v_ref, w_ref, out_ref, *, width, first):
    inner_rows(v_ref, w_ref, out_ref, width, first, out_ref.shape[0] // width, 0)


def border_kernel(core_ref, v_ref, halo_ref, w_ref, out_ref, *, width, top, bottom):
    rows = v_ref.shape[0] // width
    inner_rows(v_ref, w_ref, out_ref, width, 1, top - 1, 1)
    inner_rows(v_ref, w_ref, out_ref, width, rows - bottom, bottom - 1, top)
    core = core_ref[0]
    above = (core == 1).astype(F32)
    below = (core == 0).astype(F32)
    last = (rows - 1) * width
    for low, high in lane_tiles(out_ref.shape[1]):
        halo = halo_ref[:, low:high].astype(F32)
        taps = [halo * above] + [v_ref[d * width : (d + 1) * width, low:high].astype(F32) for d in range(2)]
        out_ref[:width, low:high] = row_branch(taps, w_ref, low, high)
        taps = [v_ref[last + d * width : last + (d + 1) * width, low:high].astype(F32) for d in (-1, 0)]
        end = (top + bottom - 1) * width
        out_ref[end : end + width, low:high] = row_branch(taps + [halo * below], w_ref, low, high)


def local_rows(kernel, number, name, order, *operands):
    width, inner = kernel.keywords["width"], operands[0].shape[1]
    return pl.pallas_call(
        kernel,
        in_specs=[SMEM] + [VMEM] * len(operands),
        out_specs=VMEM,
        out_shape=shape((number * width, inner), F32),
        compiler_params=params(4),
        cost_estimate=cost(20 * number * width * inner, 8 * number * width * inner),
        name=name,
    )(order, *operands)


def row_pieces(rows):
    top, bottom = rows // 4 - 1, 2
    upper = (rows - top - bottom + 1) // 2
    return top, bottom, upper, rows - top - bottom - upper


def halves(core, own, other):
    own, other = own.astype(F32), other.astype(F32)
    return jnp.concatenate([jnp.where(core == 0, own, other), jnp.where(core == 0, other, own)], axis=0)


def pair_matrix(state, base, pair, limit):
    block = paired(state, base, pair, limit)
    column = lax.broadcasted_iota(jnp.int32, block.shape, 1)
    top = jnp.where(column < HEAD, block, 0.0)
    bottom = jnp.where((column >= HEAD) & (column < 2 * HEAD), block, 0.0)
    rest = jnp.zeros((256 - 2 * HEAD, 256), F32)
    return jnp.concatenate([top, bottom, rest], axis=0).astype(BF16)


def head_sums():
    row = lax.broadcasted_iota(jnp.int32, (256, 256), 0)
    column = lax.broadcasted_iota(jnp.int32, (256, 256), 1)
    first = (row < HEAD) & (column < HEAD)
    second = (row >= HEAD) & (row < 2 * HEAD) & (column >= HEAD) & (column < 2 * HEAD)
    return jnp.where(first | second, 1.0, 0.0).astype(BF16)


def normed_pair(qf, matrix, sums):
    attn = matmul(qf, matrix)
    total = matmul((attn * attn).astype(BF16), sums)
    return attn * lax.rsqrt(total * (1.0 / HEAD) + 1e-06)


def placed(normed, pairs, low, high):
    tiles = {}
    for pair, block in zip(pairs, normed):
        base, offset, wide = pair_span(pair)
        if wide > 256:
            block = jnp.concatenate([block, jnp.zeros((block.shape[0], wide - 256), F32)], axis=1)
        if offset:
            block = pltpu.roll(block, offset, 1)
        for t in range(wide // 128):
            at = base + t * 128
            piece = block[:, t * 128 : (t + 1) * 128]
            tiles[at] = tiles[at] + piece if at in tiles else piece
    for at in range(low, high, 128):
        yield at, min(at + 128, high), tiles[at][:, : min(128, high - at)]


CHUNK = 320


def early_kernel(core_ref, own_ref, other_ref, qf_ref, out_ref):
    state = halves(core_ref[0], own_ref[...], other_ref[...])
    sums = head_sums()
    pairs = range(FIRST // (2 * HEAD))
    matrices = [pair_matrix(state, 0, pair, FIRST) for pair in pairs]
    for at in range(0, qf_ref.shape[0], CHUNK):
        rows = slice(at, at + CHUNK)
        normed = [normed_pair(qf_ref[rows, pair * 256 : (pair + 1) * 256], matrices[pair], sums) for pair in pairs]
        for low, high, tile in placed(normed, pairs, 0, FIRST):
            out_ref[rows, low:high] = tile


def early_heads(core, own, other, qfeat):
    count = qfeat.shape[0]
    return pl.pallas_call(
        early_kernel,
        in_specs=[SMEM] + [VMEM] * 3,
        out_specs=VMEM,
        out_shape=shape((count, FIRST), F32),
        compiler_params=params(8),
        cost_estimate=cost(4 * count * FIRST * 512, 4 * count * FIRST),
        name="early_heads",
    )(core, own, other, qfeat)


def late_kernel(
    core_ref, owna_ref, othera_ref, ownb_ref, otherb_ref, qf_ref, upper_ref, lower_ref, edge_ref, early_ref,
    gain_ref, out_hbm, out, sems, *, width
):
    core = core_ref[0]
    count, inner = out_hbm.shape
    first = FIRST // (2 * HEAD)
    low = 2 * HEAD * first // 128 * 128
    state = jnp.concatenate(
        [halves(core, owna_ref[:, low:], othera_ref[:, low:]), halves(core, ownb_ref[...], otherb_ref[...])], axis=1
    )
    sums = head_sums()
    pairs = range(first, inner // (2 * HEAD))
    matrices = [pair_matrix(state, low, pair, inner) for pair in pairs]
    top, bottom, upper, lower = (n * width for n in row_pieces(count // width))
    pieces = [
        (0, top, edge_ref, 0),
        (top, upper, upper_ref, 0),
        (top + upper, lower, lower_ref, 0),
        (count - bottom, bottom, edge_ref, top),
    ]
    copies = []
    for at in range(0, count, CHUNK):
        rows = slice(at, at + CHUNK)
        normed = [
            normed_pair(qf_ref[rows, pair * 256 : (pair + 1) * 256], matrices[pair - first], sums) for pair in pairs
        ]
        later = {a: (b, tile) for a, b, tile in placed(normed, pairs, low, inner)}
        for start, number, ref, base in pieces:
            lo, hi = max(start, at), min(start + number, at + CHUNK)
            if lo >= hi:
                continue
            here = slice(lo, hi)
            inside = slice(lo - at, hi - at)
            there = slice(lo - start + base, hi - start + base)
            for a in range(0, inner, 128):
                b, tile = later.get(a, (a + 128, None))
                value = 0.0 if tile is None else tile[inside]
                if a < FIRST:
                    value = value + early_ref[here, a:b]
                out[here, a:b] = (value * gain_ref[:, a:b] + ref[there, a:b]).astype(BF16)
            copies.append(pltpu.make_async_copy(out.at[here], out_hbm.at[here], sems.at[len(copies)]))
            copies[-1].start()
    for copy in copies:
        copy.wait()


def late_heads(core, first, second, qfeat, local, early, gain, width):
    count, inner = qfeat.shape[0], gain.shape[1]
    return pl.pallas_call(
        functools.partial(late_kernel, width=width),
        in_specs=[SMEM] + [VMEM] * 10,
        out_specs=HBM,
        scratch_shapes=[pltpu.VMEM((count, inner), BF16), pltpu.SemaphoreType.DMA((8,))],
        out_shape=shape((count, inner)),
        compiler_params=params(14),
        cost_estimate=cost(4 * count * inner * 512, 8 * count * inner),
        name="late_heads",
    )(core, *first, *second, qfeat, *local, early, gain)


def swapped(block, axis, bit):
    return lax.ppermute(block, axis, [(i, i ^ bit) for i in range(lax.axis_size(axis))])


def shards(frames_in, queries, key_weight, value_weight, conv_weight, norm_gain):
    _, rows, width, model = frames_in.shape
    inner = key_weight.shape[1]
    count = rows * width
    core = lax.axis_index("space").astype(jnp.int32).reshape(1)
    flat = frames_in.reshape(count, model)
    gain = norm_gain.reshape(1, inner)
    frame = lax.axis_index("tm")
    masks = [(frame >> b & 1).astype(F32) for b in range((lax.axis_size("tm") - 1).bit_length())]
    core, masks = lax.optimization_barrier((core, masks))

    values, mine, send, edge, q = project(
        core, flat, key_weight, value_weight, queries.reshape(count, inner), width
    )
    cuts = [slice(0, FIRST), slice(FIRST, inner)]
    sends = [send[:, cut] for cut in cuts]
    received = [swapped(part, "space", 1) for part in sends]
    halo = swapped(edge, "space", 1)
    totals = [mine[:, cut] + other.astype(F32) for cut, other in zip(cuts, received)]
    prefixes = list(totals)
    top, bottom, upper, lower = row_pieces(rows)
    middle = lambda first: functools.partial(middle_kernel, width=width, first=first)
    border = functools.partial(border_kernel, width=width, top=top, bottom=bottom)
    kernels = {
        2: lambda order: local_rows(middle(top), upper, "upper_rows", order, values, conv_weight),
        1: lambda order: local_rows(middle(top + upper), lower, "lower_rows", order, values, conv_weight),
        0: lambda order: (
            phi_queries(order, q),
            local_rows(border, top + bottom, "border_rows", order, values, halo, conv_weight),
        ),
    }
    local, qfeat = [], None
    for b, mask in enumerate(masks):
        left = len(masks) - 1 - b
        filler = kernels.get(left)
        outs = [total.astype(BF16) for total in totals]
        outs[1], order = lax.optimization_barrier((outs[1], core))
        received = [swapped(out, "tm", 1 << b) for out in outs]
        if filler is not None:
            out = filler(order)
            received[0], out = lax.optimization_barrier((received[0], out))
            if left == 0:
                qfeat, out = out
            local.append(out)
        for i, other in enumerate(received):
            other = other.astype(F32)
            prefixes[i] = prefixes[i] + mask * other
            totals[i] = totals[i] + other
    parts = [prefix.astype(BF16) for prefix in prefixes]
    others = [swapped(part, "space", 1) for part in parts]
    early = early_heads(core, parts[0], others[0], qfeat)
    others[1], early = lax.optimization_barrier((others[1], early))
    mixed = late_heads(core, (parts[0], others[0]), (parts[1], others[1]), qfeat, local, early, gain, width)
    return mixed.reshape(1, rows, width, inner)


def solution(mesh):
    in_specs = (
        P(("groups", "tm"), "space", None, None),
        P(("groups", "tm"), "space", None, None),
        P(),
        P(),
        P(),
        P(),
    )
    out_specs = P(("groups", "tm"), "space", None, None)
    return jax.shard_map(shards, mesh=mesh, in_specs=in_specs, out_specs=out_specs, check_vma=False)
```

```python
import functools

import jax
import jax.numpy as jnp
from jax import lax
from jax.experimental import pallas as pl
from jax.experimental.pallas import tpu as pltpu
from jax.sharding import PartitionSpec as P

HEAD = 112
TILE = 256
FIRST = 2 * TILE
F32 = jnp.float32
BF16 = jnp.bfloat16
MIB = 1 << 20
VMEM = pl.BlockSpec(memory_space=pltpu.VMEM)
SMEM = pl.BlockSpec(memory_space=pltpu.SMEM)


def feature_map(a):
    return jnp.maximum(a, 0.0) + jnp.exp(jnp.minimum(a, 0.0))


def matmul(a, b):
    return jnp.dot(a, b, preferred_element_type=F32)


def shape(dims, kind=BF16):
    return jax.ShapeDtypeStruct(dims, kind)


def cost(flops, moved, transcendentals=0):
    return pl.CostEstimate(flops=flops, bytes_accessed=moved, transcendentals=transcendentals)


def params(mib):
    return pltpu.CompilerParams(vmem_limit_bytes=mib * MIB)


def packed_state(keys, base, values, low):
    columns = values.shape[1]
    first, last = low // HEAD, (low + columns - 1) // HEAD
    full = matmul(keys[first * HEAD - base : (last + 1) * HEAD - base, :], values)
    column = lax.broadcasted_iota(jnp.int32, (HEAD, columns), 1) + low
    total = jnp.zeros((HEAD, columns), F32)
    for h in range(first, last + 1):
        inside = (column >= h * HEAD) & (column < (h + 1) * HEAD)
        total = total + jnp.where(inside, full[(h - first) * HEAD : (h - first + 1) * HEAD, :], 0.0)
    return total


def split_state(core, state, mine_ref, send_ref):
    half = HEAD // 2
    mine_ref[...] = state[pl.ds(pl.multiple_of(core * half, 8), half), :]
    send_ref[...] = state[pl.ds(pl.multiple_of((1 - core) * half, 8), half), :].astype(BF16)


def project_kernel(
    core_ref, x_hbm, wk_hbm, wv_hbm, q_hbm, v_ref, mine_ref, send_ref, edge_ref, q_ref,
    x_ref, tiles, ends, both, kt, state, row_sems, tile_sems, rest_sems
):
    count, inner = v_ref.shape
    width = edge_ref.shape[0]
    full = inner // TILE
    rest = inner - full * TILE
    step = count // 2
    low, high, whole = slice(0, step), slice(step, count), slice(0, count)
    rows = [
        pltpu.make_async_copy(x_hbm.at[pl.ds(i * step, step), :], x_ref.at[pl.ds(i * step, step), :], row_sems.at[i])
        for i in range(2)
    ]
    sources = [(wk_hbm, t) for t in range(full)] + [(wv_hbm, t) for t in range(full)]
    copies = [
        pltpu.make_async_copy(source.at[:, pl.ds(t * TILE, TILE)], tiles.at[i], tile_sems.at[i])
        for i, (source, t) in enumerate(sources)
    ]
    copies += [
        pltpu.make_async_copy(source.at[:, pl.ds(full * TILE, rest)], ends.at[i], rest_sems.at[i])
        for i, source in enumerate((wk_hbm, wv_hbm))
    ]
    query_copy = pltpu.make_async_copy(q_hbm, q_ref, rest_sems.at[2])

    def keys(t, here):
        kt[t * TILE : (t + 1) * TILE, here] = feature_map(matmul(x_ref[here, :], tiles[t])).astype(BF16).T

    def values(t):
        v_ref[:, t * TILE : (t + 1) * TILE] = matmul(x_ref[...], tiles[full + t]).astype(BF16)

    def states(t):
        at = slice(t * TILE, min((t + 1) * TILE, inner))
        state[:, at] = packed_state(kt, 0, v_ref[:, at], t * TILE)

    for copy in (copies[0], copies[1], *rows):
        copy.start()
    for copy in (copies[0], copies[1], rows[0]):
        copy.wait()
    for copy in copies[2:]:
        copy.start()
    keys(0, low)
    keys(1, low)
    rows[1].wait()
    query_copy.start()
    keys(0, high)
    keys(1, high)
    for copy in copies[2:]:
        copy.wait()
    both[...] = jnp.zeros_like(both)
    both[:, :rest] = ends[0]
    both[:, 128 : 128 + rest] = ends[1]
    for t in range(2, full):
        keys(t, whole)
    out = matmul(x_ref[...], both[...])
    kt[full * TILE :, :] = feature_map(out[:, :128]).astype(BF16).T[:rest, :]
    v_ref[:, full * TILE :] = out[:, 128 : 128 + rest].astype(BF16)
    for t in range(full):
        values(t)
    for t in range(full + 1):
        states(t)
    core = core_ref[0]
    split_state(core, state, mine_ref, send_ref)
    edge_ref[...] = v_ref[pl.ds(pl.multiple_of((1 - core) * (count - width), 16), width), :]
    query_copy.wait()


HBM = pl.BlockSpec(memory_space=pltpu.HBM)


def project(core, flat, key_weight, value_weight, queries, width):
    count, model = flat.shape
    inner = key_weight.shape[1]
    half = HEAD // 2
    full = inner // TILE
    return pl.pallas_call(
        project_kernel,
        in_specs=[SMEM] + [HBM] * 4,
        out_specs=[VMEM] * 5,
        scratch_shapes=[
            pltpu.VMEM((count, model), BF16),
            pltpu.VMEM((2 * full, model, TILE), BF16),
            pltpu.VMEM((2, model, inner - full * TILE), BF16),
            pltpu.VMEM((model, TILE), BF16),
            pltpu.VMEM((inner, count), BF16),
            pltpu.VMEM((HEAD, inner), F32),
            pltpu.SemaphoreType.DMA((2,)),
            pltpu.SemaphoreType.DMA((2 * full,)),
            pltpu.SemaphoreType.DMA((3,)),
        ],
        out_shape=[
            shape((count, inner)),
            shape((half, inner), F32),
            shape((half, inner)),
            shape((width, inner)),
            shape((count, inner)),
        ],
        compiler_params=params(30),
        cost_estimate=cost(4 * count * model * inner, 2 * model * (count + 2 * inner)),
        name="project",
    )(core, *(pltpu.with_memory_space_constraint(a, pltpu.HBM) for a in (flat, key_weight, value_weight, queries)))


def pair_span(pair):
    start = 2 * HEAD * pair
    base = start // 128 * 128
    return base, start - base, 256 if start - base + 2 * HEAD <= 256 else 384


def paired(block, base, pair, limit):
    low, offset, wide = pair_span(pair)
    piece = block[:, low - base : min(low + wide, limit) - base]
    if piece.shape[1] < wide:
        piece = jnp.concatenate([piece, jnp.zeros((piece.shape[0], wide - piece.shape[1]), piece.dtype)], axis=1)
    if offset:
        piece = pltpu.roll(piece, wide - offset, 1)
    return piece[:, :256]


def phi_kernel(order_ref, q_ref, qf_ref):
    inner = q_ref.shape[1]
    step = 160

    def rows(i, carry):
        here = pl.ds(pl.multiple_of(i * step, 16), step)
        for pair in range(inner // (2 * HEAD)):
            low, _, wide = pair_span(pair)
            q = feature_map(q_ref[here, low : min(low + wide, inner)].astype(F32)).astype(BF16)
            qf_ref[here, pair * 256 : (pair + 1) * 256] = paired(q, low, pair, inner)
        return carry

    lax.fori_loop(0, q_ref.shape[0] // step, rows, 0)


def phi_queries(order, queries):
    count, inner = queries.shape
    pairs = inner // (2 * HEAD)
    return pl.pallas_call(
        phi_kernel,
        in_specs=[SMEM, VMEM],
        out_specs=VMEM,
        out_shape=shape((count, pairs * 256)),
        compiler_params=params(4),
        cost_estimate=cost(8 * count * inner, 4 * count * inner, count * inner),
        name="phi_queries",
    )(order, queries)


def row_branch(taps, w_ref, low, high):
    side = []
    for c in range(3):
        acc = taps[0] * w_ref[c : c + 1, low:high]
        acc = acc + taps[1] * w_ref[3 + c : 4 + c, low:high]
        side.append(acc + taps[2] * w_ref[6 + c : 7 + c, low:high])
    width = side[0].shape[0]
    place = lax.broadcasted_iota(jnp.int32, side[0].shape, 0)
    left = jnp.where(place > 0, pltpu.roll(side[0], 1, 0), 0.0)
    right = jnp.where(place < width - 1, pltpu.roll(side[2], width - 1, 0), 0.0)
    return side[1] + left + right


def lane_tiles(inner):
    return [(low, min(low + 128, inner)) for low in range(0, inner, 128)]


def inner_rows(v_ref, w_ref, out_ref, width, first, number, at):

    def row(r, carry):
        here = pl.ds(pl.multiple_of((at + r) * width, 16), width)
        for low, high in lane_tiles(out_ref.shape[1]):
            taps = [
                v_ref[pl.ds(pl.multiple_of((first + r + d - 1) * width, 16), width), low:high].astype(F32)
                for d in range(3)
            ]
            out_ref[here, low:high] = row_branch(taps, w_ref, low, high)
        return carry

    lax.fori_loop(0, number, row, 0)


def middle_kernel(order_ref, v_ref, w_ref, out_ref, *, width, first):
    inner_rows(v_ref, w_ref, out_ref, width, first, out_ref.shape[0] // width, 0)


def border_kernel(core_ref, v_ref, halo_ref, w_ref, out_ref, *, width, top, bottom):
    rows = v_ref.shape[0] // width
    inner_rows(v_ref, w_ref, out_ref, width, 1, top - 1, 1)
    inner_rows(v_ref, w_ref, out_ref, width, rows - bottom, bottom - 1, top)
    core = core_ref[0]
    above = (core == 1).astype(F32)
    below = (core == 0).astype(F32)
    last = (rows - 1) * width
    for low, high in lane_tiles(out_ref.shape[1]):
        halo = halo_ref[:, low:high].astype(F32)
        taps = [halo * above] + [v_ref[d * width : (d + 1) * width, low:high].astype(F32) for d in range(2)]
        out_ref[:width, low:high] = row_branch(taps, w_ref, low, high)
        taps = [v_ref[last + d * width : last + (d + 1) * width, low:high].astype(F32) for d in (-1, 0)]
        end = (top + bottom - 1) * width
        out_ref[end : end + width, low:high] = row_branch(taps + [halo * below], w_ref, low, high)


def local_rows(kernel, number, name, order, *operands):
    width, inner = kernel.keywords["width"], operands[0].shape[1]
    return pl.pallas_call(
        kernel,
        in_specs=[SMEM] + [VMEM] * len(operands),
        out_specs=VMEM,
        out_shape=shape((number * width, inner), F32),
        compiler_params=params(4),
        cost_estimate=cost(20 * number * width * inner, 8 * number * width * inner),
        name=name,
    )(order, *operands)


def row_pieces(rows):
    top, bottom = rows // 8, 2
    upper = (rows - top - bottom + 1) // 2
    return top, bottom, upper, rows - top - bottom - upper


def halves(core, own, other):
    own, other = own.astype(F32), other.astype(F32)
    return jnp.concatenate([jnp.where(core == 0, own, other), jnp.where(core == 0, other, own)], axis=0)


def pair_matrix(state, base, pair, limit):
    block = paired(state, base, pair, limit)
    column = lax.broadcasted_iota(jnp.int32, block.shape, 1)
    top = jnp.where(column < HEAD, block, 0.0)
    bottom = jnp.where((column >= HEAD) & (column < 2 * HEAD), block, 0.0)
    rest = jnp.zeros((256 - 2 * HEAD, 256), F32)
    return jnp.concatenate([top, bottom, rest], axis=0).astype(BF16)


def head_sums():
    row = lax.broadcasted_iota(jnp.int32, (256, 256), 0)
    column = lax.broadcasted_iota(jnp.int32, (256, 256), 1)
    first = (row < HEAD) & (column < HEAD)
    second = (row >= HEAD) & (row < 2 * HEAD) & (column >= HEAD) & (column < 2 * HEAD)
    return jnp.where(first | second, 1.0, 0.0).astype(BF16)


def normed_pair(qf, matrix, sums):
    attn = matmul(qf, matrix)
    total = matmul((attn * attn).astype(BF16), sums)
    return attn * lax.rsqrt(total * (1.0 / HEAD) + 1e-06)


def placed(normed, pairs, low, high):
    tiles = {}
    for pair, block in zip(pairs, normed):
        base, offset, wide = pair_span(pair)
        if wide > 256:
            block = jnp.concatenate([block, jnp.zeros((block.shape[0], wide - 256), F32)], axis=1)
        if offset:
            block = pltpu.roll(block, offset, 1)
        for t in range(wide // 128):
            at = base + t * 128
            piece = block[:, t * 128 : (t + 1) * 128]
            tiles[at] = tiles[at] + piece if at in tiles else piece
    for at in range(low, high, 128):
        yield at, min(at + 128, high), tiles[at][:, : min(128, high - at)]


CHUNK = 320


def early_kernel(core_ref, own_ref, other_ref, qf_ref, out_ref):
    state = halves(core_ref[0], own_ref[...], other_ref[...])
    sums = head_sums()
    pairs = range(FIRST // (2 * HEAD))
    matrices = [pair_matrix(state, 0, pair, FIRST) for pair in pairs]
    for at in range(0, qf_ref.shape[0], CHUNK):
        rows = slice(at, at + CHUNK)
        normed = [normed_pair(qf_ref[rows, pair * 256 : (pair + 1) * 256], matrices[pair], sums) for pair in pairs]
        for low, high, tile in placed(normed, pairs, 0, FIRST):
            out_ref[rows, low:high] = tile


def early_heads(core, own, other, qfeat):
    count = qfeat.shape[0]
    return pl.pallas_call(
        early_kernel,
        in_specs=[SMEM] + [VMEM] * 3,
        out_specs=VMEM,
        out_shape=shape((count, FIRST), F32),
        compiler_params=params(8),
        cost_estimate=cost(4 * count * FIRST * 512, 4 * count * FIRST),
        name="early_heads",
    )(core, own, other, qfeat)


def late_kernel(
    core_ref, owna_ref, othera_ref, ownb_ref, otherb_ref, qf_ref, upper_ref, lower_ref, edge_ref, early_ref,
    gain_ref, out_hbm, out, sems, *, width
):
    core = core_ref[0]
    count, inner = out_hbm.shape
    first = FIRST // (2 * HEAD)
    low = 2 * HEAD * first // 128 * 128
    state = jnp.concatenate(
        [halves(core, owna_ref[:, low:], othera_ref[:, low:]), halves(core, ownb_ref[...], otherb_ref[...])], axis=1
    )
    sums = head_sums()
    pairs = range(first, inner // (2 * HEAD))
    matrices = [pair_matrix(state, low, pair, inner) for pair in pairs]
    top, bottom, upper, lower = (n * width for n in row_pieces(count // width))
    pieces = [
        (0, top, edge_ref, 0),
        (top, upper, upper_ref, 0),
        (top + upper, lower, lower_ref, 0),
        (count - bottom, bottom, edge_ref, top),
    ]
    copies = []
    for at in range(0, count, CHUNK):
        rows = slice(at, at + CHUNK)
        normed = [
            normed_pair(qf_ref[rows, pair * 256 : (pair + 1) * 256], matrices[pair - first], sums) for pair in pairs
        ]
        later = {a: (b, tile) for a, b, tile in placed(normed, pairs, low, inner)}
        for start, number, ref, base in pieces:
            lo, hi = max(start, at), min(start + number, at + CHUNK)
            if lo >= hi:
                continue
            here = slice(lo, hi)
            inside = slice(lo - at, hi - at)
            there = slice(lo - start + base, hi - start + base)
            for a in range(0, inner, 128):
                b, tile = later.get(a, (a + 128, None))
                value = 0.0 if tile is None else tile[inside]
                if a < FIRST:
                    value = value + early_ref[here, a:b]
                out[here, a:b] = (value * gain_ref[:, a:b] + ref[there, a:b]).astype(BF16)
            copies.append(pltpu.make_async_copy(out.at[here], out_hbm.at[here], sems.at[len(copies)]))
            copies[-1].start()
    for copy in copies:
        copy.wait()


def late_heads(core, first, second, qfeat, local, early, gain, width):
    count, inner = qfeat.shape[0], gain.shape[1]
    return pl.pallas_call(
        functools.partial(late_kernel, width=width),
        in_specs=[SMEM] + [VMEM] * 10,
        out_specs=HBM,
        scratch_shapes=[pltpu.VMEM((count, inner), BF16), pltpu.SemaphoreType.DMA((8,))],
        out_shape=shape((count, inner)),
        compiler_params=params(14),
        cost_estimate=cost(4 * count * inner * 512, 8 * count * inner),
        name="late_heads",
    )(core, *first, *second, qfeat, *local, early, gain)


def swapped(block, axis, bit):
    return lax.ppermute(block, axis, [(i, i ^ bit) for i in range(lax.axis_size(axis))])


def shards(frames_in, queries, key_weight, value_weight, conv_weight, norm_gain):
    _, rows, width, model = frames_in.shape
    inner = key_weight.shape[1]
    count = rows * width
    core = lax.axis_index("space").astype(jnp.int32).reshape(1)
    flat = frames_in.reshape(count, model)
    gain = norm_gain.reshape(1, inner)
    frame = lax.axis_index("tm")
    masks = [(frame >> b & 1).astype(F32) for b in range((lax.axis_size("tm") - 1).bit_length())]
    core, masks = lax.optimization_barrier((core, masks))

    values, mine, send, edge, q = project(
        core, flat, key_weight, value_weight, queries.reshape(count, inner), width
    )
    cuts = [slice(0, FIRST), slice(FIRST, inner)]
    sends = [send[:, cut] for cut in cuts]
    received = [swapped(part, "space", 1) for part in sends]
    halo = swapped(edge, "space", 1)
    totals = [mine[:, cut] + other.astype(F32) for cut, other in zip(cuts, received)]
    prefixes = list(totals)
    top, bottom, upper, lower = row_pieces(rows)
    middle = lambda first: functools.partial(middle_kernel, width=width, first=first)
    border = functools.partial(border_kernel, width=width, top=top, bottom=bottom)
    kernels = {
        2: lambda order: local_rows(middle(top), upper, "upper_rows", order, values, conv_weight),
        1: lambda order: local_rows(middle(top + upper), lower, "lower_rows", order, values, conv_weight),
        0: lambda order: (
            phi_queries(order, q),
            local_rows(border, top + bottom, "border_rows", order, values, halo, conv_weight),
        ),
    }
    local, qfeat = [], None
    for b, mask in enumerate(masks):
        left = len(masks) - 1 - b
        filler = kernels.get(left)
        outs = [total.astype(BF16) for total in totals]
        outs[1], order = lax.optimization_barrier((outs[1], core))
        received = [swapped(out, "tm", 1 << b) for out in outs]
        if filler is not None:
            out = filler(order)
            received[0], out = lax.optimization_barrier((received[0], out))
            if left == 0:
                qfeat, out = out
            local.append(out)
        for i, other in enumerate(received):
            other = other.astype(F32)
            prefixes[i] = prefixes[i] + mask * other
            totals[i] = totals[i] + other
    parts = [prefix.astype(BF16) for prefix in prefixes]
    others = [swapped(part, "space", 1) for part in parts]
    early = early_heads(core, parts[0], others[0], qfeat)
    others[1], early = lax.optimization_barrier((others[1], early))
    mixed = late_heads(core, (parts[0], others[0]), (parts[1], others[1]), qfeat, local, early, gain, width)
    return mixed.reshape(1, rows, width, inner)


def solution(mesh):
    in_specs = (
        P(("groups", "tm"), "space", None, None),
        P(("groups", "tm"), "space", None, None),
        P(),
        P(),
        P(),
        P(),
    )
    out_specs = P(("groups", "tm"), "space", None, None)
    return jax.shard_map(shards, mesh=mesh, in_specs=in_specs, out_specs=out_specs, check_vma=False)
```
